256 devices in a mesh: ta: 8 (over y_hi, x), xyz: 32 (over z, y_lo, core).
Axes of the slice: x: 4, y: 4 (y_hi: 2, y_lo: 2; y = y_hi * 2 + y_lo), z: 8, core: 2. Of those that a mesh axis runs over, the one named last changes fastest.
Arguments:
- gauge: float32 [4, 2, 3, 3, 16, 32, 1, 512], P(None, None, None, None, 'ta', 'xyz'), may hold values from -2.4 to 2.4
- clover_inverse: bfloat16 [2, 2, 6, 6, 16, 32, 1, 512], P(None, None, None, None, 'ta', 'xyz'), may hold values from -0.61 to 1
- source: float32 [2, 4, 3, 16, 32, 1, 512], P(None, None, None, 'ta', 'xyz'), may hold values from -6 to 6
- xi: float32 [2, 4, 3, 16, 32, 1, 512], P(None, None, None, 'ta', 'xyz'), may hold values from -6 to 6
- eta: float32 [2, 4, 3, 16, 32, 1, 512], P(None, None, None, 'ta', 'xyz'), may hold values from -6 to 6
- momentum: float32 [4, 2, 3, 3, 16, 32, 1, 512], P(None, None, None, None, 'ta', 'xyz'), may hold values from -6 to 6
Outputs:
- solution: float32 [2, 4, 3, 16, 32, 1, 512], P(None, None, None, 'ta', 'xyz')
- new_momentum: float32 [4, 2, 3, 3, 16, 32, 1, 512], P(None, None, None, None, 'ta', 'xyz')
The draws below stay inside these ranges and needn't reach their ends.
All inputs are finite; a program needn't handle non-finite values.
Results may differ from the reference program's by a relative error of at most 0.022.
Values may be sent and summed in bfloat16 or wider, within the bound.
A program may use at most 64 MiB of HBM per device.

```python
import jax
import jax.numpy as jnp
from jax import lax

LX = 1
LY = 8
NZ = 64
ITERS = 8
NT = 16
BLOCKS = 32
NX = 32
N_XYZ = 32


def draw_clover_inverse(key, part):
    shape = (2, 2, 6, 6, NT, BLOCKS, LX, LY * NZ)
    key_diag = jax.random.fold_in(key, 11)
    key_off = jax.random.fold_in(key, 23)
    diagonal = jax.random.uniform(key_diag, shape, jnp.float32, 0.6, 1.0)
    offdiag = jnp.clip(0.15 * jax.random.normal(key_off, shape, jnp.float32), -0.6, 0.6)
    identity = jnp.eye(6, dtype=jnp.float32).reshape((1, 1, 6, 6, 1, 1, 1, 1))
    real_mask = jnp.array([1.0, 0.0], jnp.float32).reshape((1, 2, 1, 1, 1, 1, 1, 1))
    values = identity * real_mask * diagonal + (1.0 - identity) * offdiag
    return values.astype(jnp.bfloat16)


def block_scale(rng, extent, shards, smallest, top_value):
    loudness = 1.0
    for position, shards_of in shards:
        draws = jax.random.uniform(jax.random.fold_in(jax.random.fold_in(rng, 6), position), (shards_of,), jnp.float32, smallest / len(shards), top_value / len(shards))
        loudness = loudness * jnp.repeat(jnp.exp(draws), extent[position] // shards_of).reshape((-1,) + (1,) * (len(extent) - 1 - position))
    return loudness


def normal_values(key, shape, spread, bound, shards=(), kind=jnp.bfloat16):
    result = spread * jax.random.normal(key, shape, jnp.float32)
    if shards:
        result = result * block_scale(key, shape, shards, -0.22, 0.18)
    return jnp.clip(result, -bound, bound).astype(kind)


def setup_inputs(seed: int = 0) -> dict:
    key_of = jax.random.split(jax.random.key(seed), 7)
    gauge = normal_values(key_of[0], (4, 2, 3, 3, NT, BLOCKS, LX, LY * NZ), 0.4, 2.4, ((4, 8), (5, 32)), jnp.float32)
    clover_inverse = draw_clover_inverse(jax.random.fold_in(key_of[6], 71), 0)
    source = normal_values(key_of[2], (2, 4, 3, NT, BLOCKS, LX, LY * NZ), 1.0, 6.0, ((3, 8), (4, 32)), jnp.float32)
    xi = normal_values(key_of[3], (2, 4, 3, NT, BLOCKS, LX, LY * NZ), 1.0, 6.0, ((3, 8), (4, 32)), jnp.float32)
    eta = normal_values(key_of[4], (2, 4, 3, NT, BLOCKS, LX, LY * NZ), 1.0, 6.0, ((3, 8), (4, 32)), jnp.float32)
    momentum = normal_values(key_of[5], (4, 2, 3, 3, NT, BLOCKS, LX, LY * NZ), 1.0, 6.0, ((4, 8), (5, 32)), jnp.float32)
    return dict(gauge=gauge, clover_inverse=clover_inverse, source=source, xi=xi, eta=eta, momentum=momentum)


hop_scale = 0.18
step_size = 0.25


def rounded(values):
    return lax.optimization_barrier(values.astype(jnp.bfloat16)).astype(jnp.float32)


def to_grid(field):
    lead = field.shape[:-4]
    return field.reshape(lead + (NT, NX, LY, NZ))


def from_grid(field):
    lead = field.shape[:-4]
    return field.reshape(lead + (NT, N_XYZ, LX, LY * NZ))


def neighbour(field, direction, offset):
    return jnp.roll(field, -offset, axis=field.ndim - 4 + direction)


def rotate(direction, sign, real_part, imag_part):
    if direction == 0:
        return sign * real_part, sign * imag_part
    if direction == 1:
        sig_real = real_part[::-1]
        sig_imag = imag_part[::-1]
    elif direction == 2:
        sig_real = jnp.stack([imag_part[1], -imag_part[0]])
        sig_imag = jnp.stack([-real_part[1], real_part[0]])
    else:
        sig_real = jnp.stack([real_part[0], -real_part[1]])
        sig_imag = jnp.stack([imag_part[0], -imag_part[1]])
    return -sign * sig_imag, sign * sig_real


def project(direction, sign, spinor):
    inverse_sign = sign if direction == 0 else -sign
    lower_real, lower_imag = rotate(direction, inverse_sign, spinor[0, 2:], spinor[1, 2:])
    return jnp.stack([spinor[0, :2] + lower_real, spinor[1, :2] + lower_imag])


def expand(direction, sign, half_spinor):
    lower_real, lower_imag = rotate(direction, sign, half_spinor[0], half_spinor[1])
    return jnp.concatenate([half_spinor, jnp.stack([lower_real, lower_imag])], axis=1)


def colour_apply(matrix, vector):
    mat_real = matrix[0][None]
    mat_imag = matrix[1][None]
    vec_real = vector[0][:, None]
    vec_imag = vector[1][:, None]
    real_part = jnp.sum(mat_real * vec_real - mat_imag * vec_imag, axis=2)
    imag_part = jnp.sum(mat_real * vec_imag + mat_imag * vec_real, axis=2)
    return jnp.stack([real_part, imag_part])


def dagger(matrix):
    return jnp.stack([jnp.swapaxes(matrix[0], 0, 1), -jnp.swapaxes(matrix[1], 0, 1)])


def colour_product(left, right):
    left_real = left[0][:, :, None]
    left_imag = left[1][:, :, None]
    right_real = right[0][None]
    right_imag = right[1][None]
    real_part = jnp.sum(left_real * right_real - left_imag * right_imag, axis=1)
    imag_part = jnp.sum(left_real * right_imag + left_imag * right_real, axis=1)
    return jnp.stack([real_part, imag_part])


def outer_sum(left, right):
    left_real = left[0][:, :, None]
    left_imag = left[1][:, :, None]
    right_real = right[0][:, None]
    right_imag = right[1][:, None]
    real_part = jnp.sum(left_real * right_real + left_imag * right_imag, axis=0)
    imag_part = jnp.sum(left_imag * right_real - left_real * right_imag, axis=0)
    return jnp.stack([real_part, imag_part])


def traceless(force):
    real_part = 0.5 * (force[0] - jnp.swapaxes(force[0], 0, 1))
    imag_part = 0.5 * (force[1] + jnp.swapaxes(force[1], 0, 1))
    trace = (force[1, 0, 0] + force[1, 1, 1] + force[1, 2, 2]) / 3.0
    identity = jnp.eye(3, dtype=jnp.float32).reshape((3, 3) + (1,) * (force.ndim - 3))
    return jnp.stack([real_part, imag_part - identity * trace])


def clover_apply(blocks, vector):
    parts = []
    for chiral in range(2):
        piece = vector[:, 2 * chiral:2 * chiral + 2].reshape((2, 6) + vector.shape[3:])
        block_real = blocks[chiral, 0].astype(jnp.float32)
        block_imag = blocks[chiral, 1].astype(jnp.float32)
        real_part = jnp.sum(block_real * piece[0][None] - block_imag * piece[1][None], axis=1)
        imag_part = jnp.sum(block_real * piece[1][None] + block_imag * piece[0][None], axis=1)
        parts.append(jnp.stack([real_part, imag_part]).reshape((2, 2, 3) + vector.shape[3:]))
    return jnp.concatenate(parts, axis=1)


def hopping(spinor, links):
    total = jnp.zeros(spinor.shape, jnp.float32)
    for direction in range(4):
        ahead = rounded(project(direction, -1.0, neighbour(spinor, direction, 1)))
        behind = rounded(project(direction, 1.0, neighbour(spinor, direction, -1)))
        back_link = dagger(neighbour(links[direction], direction, -1))
        total = total + expand(direction, -1.0, colour_apply(links[direction], ahead))
        total = total + expand(direction, 1.0, colour_apply(back_link, behind))
    return total


def reference(gauge, clover_inverse, source, xi, eta, momentum):
    gauge = to_grid(gauge)
    clover_inverse = to_grid(clover_inverse)
    source = to_grid(source)
    xi = to_grid(xi)
    eta = to_grid(eta)
    momentum = to_grid(momentum)
    links = rounded(gauge)
    solution = clover_apply(clover_inverse, rounded(source))
    for iteration in range(ITERS):
        spinor = rounded(solution)
        solution = clover_apply(clover_inverse, rounded(source + hop_scale * hopping(spinor, links)))
    updated = []
    for direction in range(4):
        ahead_eta = neighbour(eta, direction, 1)
        ahead_xi = neighbour(xi, direction, 1)
        outer = outer_sum(expand(direction, -1.0, project(direction, -1.0, ahead_eta)), xi)
        outer = outer + outer_sum(expand(direction, 1.0, project(direction, 1.0, ahead_xi)), eta)
        force = colour_product(gauge[direction], outer)
        updated.append(momentum[direction] - step_size * traceless(force))
    return from_grid(solution), from_grid(jnp.stack(updated))
```

```python
import functools

import jax
import jax.numpy as jnp
from jax import lax
from jax.experimental import pallas as pl
from jax.experimental.pallas import tpu as pltpu
from jax.sharding import PartitionSpec as P

NZ = 64
ITERS = 8

hop_scale = 0.18
step_size = 0.25

ROWS = 8
LANES = 128
SLICE = 4


def combine(base, sign, term):
    return base + term if sign > 0 else base - term


def rotated(direction, sign, real, imag):
    if direction == 0:
        return [(sign, real[0]), (sign, real[1])], [(sign, imag[0]), (sign, imag[1])]
    if direction == 1:
        sig_real = [(1, real[1]), (1, real[0])]
        sig_imag = [(1, imag[1]), (1, imag[0])]
    elif direction == 2:
        sig_real = [(1, imag[1]), (-1, imag[0])]
        sig_imag = [(-1, real[1]), (1, real[0])]
    else:
        sig_real = [(1, real[0]), (-1, real[1])]
        sig_imag = [(1, imag[0]), (-1, imag[1])]
    return [(-sign * s, v) for s, v in sig_imag], [(sign * s, v) for s, v in sig_real]


def project(direction, sign, spinor):
    inverse_sign = sign if direction == 0 else -sign
    lower_real, lower_imag = rotated(
        direction, inverse_sign, [spinor[0, 2], spinor[0, 3]], [spinor[1, 2], spinor[1, 3]]
    )
    real = [combine(spinor[0, s], *lower_real[s]) for s in range(2)]
    imag = [combine(spinor[1, s], *lower_imag[s]) for s in range(2)]
    return real, imag


def add_expanded(total, direction, sign, half):
    real, imag = half
    lower_real, lower_imag = rotated(direction, sign, real, imag)
    new_real = [total[0][s] + real[s] for s in range(2)]
    new_real += [combine(total[0][2 + s], *lower_real[s]) for s in range(2)]
    new_imag = [total[1][s] + imag[s] for s in range(2)]
    new_imag += [combine(total[1][2 + s], *lower_imag[s]) for s in range(2)]
    return [new_real, new_imag]


def link_apply(links, direction, half):
    real, imag = half
    out_real, out_imag = [None, None], [None, None]
    for b in range(3):
        mat_real = links[direction, 0, :, b]
        mat_imag = links[direction, 1, :, b]
        for s in range(2):
            vec_real, vec_imag = real[s][b : b + 1], imag[s][b : b + 1]
            part_real = mat_real * vec_real - mat_imag * vec_imag
            part_imag = mat_real * vec_imag + mat_imag * vec_real
            out_real[s] = part_real if b == 0 else out_real[s] + part_real
            out_imag[s] = part_imag if b == 0 else out_imag[s] + part_imag
    return out_real, out_imag


def dagger_apply(links, direction, half):
    real, imag = half
    out_real, out_imag = [None, None], [None, None]
    for b in range(3):
        mat_real = links[direction, 0, b]
        mat_imag = links[direction, 1, b]
        for s in range(2):
            vec_real, vec_imag = real[s][b : b + 1], imag[s][b : b + 1]
            part_real = mat_real * vec_real + mat_imag * vec_imag
            part_imag = mat_real * vec_imag - mat_imag * vec_real
            out_real[s] = part_real if b == 0 else out_real[s] + part_real
            out_imag[s] = part_imag if b == 0 else out_imag[s] + part_imag
    return out_real, out_imag


def row_of(shape):
    return lax.broadcasted_iota(jnp.int32, shape, len(shape) - 2)


def lane_of(shape):
    return lax.broadcasted_iota(jnp.int32, shape, len(shape) - 1)


def roll(x, shift, axis):
    return pltpu.roll(x, shift, axis=x.ndim - 2 + axis)


def swap_slices(x):
    return roll(x, SLICE, 0)


def ahead_of(direction, x):
    if direction == 3:
        last = lane_of(x.shape) % NZ == NZ - 1
        return jnp.where(last, roll(x, NZ - 1, 1), roll(x, LANES - 1, 1))
    halves = roll(x, NZ, 1)
    row = row_of(x.shape) % SLICE
    next_pair = jnp.where(row == SLICE - 1, roll(halves, SLICE - 1, 0), roll(halves, ROWS - 1, 0))
    return jnp.where(lane_of(x.shape) < NZ, halves, next_pair)


def behind_of(direction, x):
    if direction == 3:
        first = lane_of(x.shape) % NZ == 0
        return jnp.where(first, roll(x, LANES - NZ + 1, 1), roll(x, 1, 1))
    halves = roll(x, NZ, 1)
    row = row_of(x.shape) % SLICE
    last_pair = jnp.where(row == 0, roll(halves, ROWS - SLICE + 1, 0), roll(halves, 1, 0))
    return jnp.where(lane_of(x.shape) < NZ, last_pair, halves)


def both_spins(half):
    return [jnp.concatenate(part, axis=0) for part in half]


def two_spins(real, imag):
    return [real[:3], real[3:]], [imag[:3], imag[3:]]


def to_bf16(x):
    return x.reshape(x.shape[0] // 2, 2 * ROWS, LANES).astype(jnp.bfloat16)


def to_f32(x):
    return x.astype(jnp.float32).reshape(2 * x.shape[0], ROWS, LANES)


def first_slice(real, imag):
    return jnp.where(row_of(real.shape) < SLICE, real, swap_slices(imag))


def last_slice(real, imag):
    return jnp.where(row_of(real.shape) < SLICE, swap_slices(real), imag)


def kernel(
    gauge_hbm, clover_hbm, source_hbm, xi_hbm, eta_hbm, momentum_hbm,
    solution_hbm, updated_hbm,
    gauge, clover_low, source, xi, eta, momentum,
    links, clover, psi, total, updated, t_ahead_local, t_behind_local,
    t_minus, t_plus, x_minus, x_plus,
    t_ahead, t_behind, x_ahead, x_behind,
    rim_t, rim_x, rim_t_ahead, rim_x_ahead,
    load_sem, store_sem, send_sem, recv_sem, rim_send_sem, rim_recv_sem,
):
    n_t, n_x = lax.axis_size("ta"), lax.axis_size("xyz")
    my_t, my_x = lax.axis_index("ta"), lax.axis_index("xyz")
    t_next, t_last = {"ta": lax.rem(my_t + 1, n_t)}, {"ta": lax.rem(my_t + n_t - 1, n_t)}
    x_next, x_last = {"xyz": lax.rem(my_x + 1, n_x)}, {"xyz": lax.rem(my_x + n_x - 1, n_x)}

    barrier = pltpu.get_barrier_semaphore()
    for device in (t_next, t_last, x_next, x_last):
        pl.semaphore_signal(barrier, inc=1, device_id=device, device_id_type=pl.DeviceIdType.MESH)

    loads = [
        pltpu.make_async_copy(src, dst, load_sem.at[i])
        for i, (src, dst) in enumerate([
            (source_hbm, source), (clover_hbm, clover_low), (gauge_hbm, gauge),
            (xi_hbm, xi), (eta_hbm, eta), (momentum_hbm, momentum),
        ])
    ]
    for load in loads:
        load.start()

    def remote(src, dst, send, recv, device):
        return pltpu.make_async_remote_copy(
            src_ref=src, dst_ref=dst, send_sem=send, recv_sem=recv,
            device_id=device, device_id_type=pl.DeviceIdType.MESH,
        )

    def halo_copies(slot):
        return [
            remote(src.at[slot], dst.at[slot], send_sem.at[i, slot], recv_sem.at[i, slot], device)
            for i, (src, dst, device) in enumerate([
                (t_minus, t_ahead, t_last), (t_plus, t_behind, t_next),
                (x_minus, x_ahead, x_last), (x_plus, x_behind, x_next),
            ])
        ]

    def rim_copies():
        return [
            remote(rim_t, rim_t_ahead, rim_send_sem.at[0], rim_recv_sem.at[0], t_last),
            remote(rim_x, rim_x_ahead, rim_send_sem.at[1], rim_recv_sem.at[1], x_last),
        ]

    def clover_apply(vector):
        for chiral in range(2):
            out_real = out_imag = None
            for j in range(6):
                spin, colour = 2 * chiral + j // 3, j % 3
                vec_real = vector[0][spin][colour : colour + 1]
                vec_imag = vector[1][spin][colour : colour + 1]
                mat_real = clover[chiral, 0, :, j]
                mat_imag = clover[chiral, 1, :, j]
                part_real = mat_real * vec_real - mat_imag * vec_imag
                part_imag = mat_real * vec_imag + mat_imag * vec_real
                out_real = part_real if j == 0 else out_real + part_real
                out_imag = part_imag if j == 0 else out_imag + part_imag
            for s in range(2):
                psi[0, 2 * chiral + s] = out_real[3 * s : 3 * s + 3]
                psi[1, 2 * chiral + s] = out_imag[3 * s : 3 * s + 3]

    def send_halos(slot):
        copies = halo_copies(slot)
        real, imag = both_spins(project(0, -1, psi))
        t_minus[slot] = to_bf16(first_slice(real, imag))
        copies[0].start()
        t_ahead_local[0] = swap_slices(real)
        t_ahead_local[1] = swap_slices(imag)
        real, imag = both_spins(dagger_apply(links, 0, project(0, 1, psi)))
        t_plus[slot] = to_bf16(last_slice(real, imag))
        copies[1].start()
        t_behind_local[0] = swap_slices(real)
        t_behind_local[1] = swap_slices(imag)
        x_minus[slot] = to_bf16(jnp.concatenate(both_spins(project(1, -1, psi)), axis=0))
        copies[2].start()
        x_plus[slot] = to_bf16(
            jnp.concatenate(both_spins(dagger_apply(links, 1, project(1, 1, psi))), axis=0)
        )
        copies[3].start()

    def read_total(ref):
        return [[ref[part, s] for s in range(4)] for part in range(2)]

    def local_hops():
        result = read_total(source)
        for direction in (2, 3):
            half = both_spins(project(direction, -1, psi))
            half = two_spins(*[ahead_of(direction, part) for part in half])
            result = add_expanded(result, direction, -1, link_apply(links, direction, half))
            half = both_spins(dagger_apply(links, direction, project(direction, 1, psi)))
            half = two_spins(*[behind_of(direction, part) for part in half])
            result = add_expanded(result, direction, 1, half)
        for part in range(2):
            for s in range(4):
                total[part, s] = result[part][s]

    def receive_halos(slot):
        copies = halo_copies(slot)
        result = read_total(total)
        copies[2].wait_recv()
        half = to_f32(x_ahead[slot])
        result = add_expanded(result, 1, -1, link_apply(links, 1, two_spins(half[:6], half[6:])))
        copies[3].wait_recv()
        half = to_f32(x_behind[slot])
        result = add_expanded(result, 1, 1, two_spins(half[:6], half[6:]))
        copies[0].wait_recv()
        rim = to_f32(t_ahead[slot])
        first = row_of(rim.shape) < SLICE
        half = two_spins(
            jnp.where(first, t_ahead_local[0], swap_slices(rim)), jnp.where(first, t_ahead_local[1], rim)
        )
        result = add_expanded(result, 0, -1, link_apply(links, 0, half))
        copies[1].wait_recv()
        rim = to_f32(t_behind[slot])
        half = two_spins(
            jnp.where(first, rim, t_behind_local[0]), jnp.where(first, swap_slices(rim), t_behind_local[1])
        )
        return add_expanded(result, 0, 1, half)

    def send_rims():
        copies = rim_copies()
        for i, (sign, field) in enumerate([(1, xi), (-1, eta)]):
            real, imag = both_spins(project(0, sign, field))
            rim_t[i] = first_slice(real, imag)
            real, imag = both_spins(project(1, sign, field))
            rim_x[i, 0] = real
            rim_x[i, 1] = imag
        for copy in copies:
            copy.start()

    def half_ahead(direction, sign, field, index):
        if direction == 1:
            return two_spins(rim_x_ahead[index, 0], rim_x_ahead[index, 1])
        real, imag = both_spins(project(direction, sign, field))
        if direction == 0:
            rim = rim_t_ahead[index]
            first = row_of(rim.shape) < SLICE
            real = jnp.where(first, swap_slices(real), swap_slices(rim))
            imag = jnp.where(first, swap_slices(imag), rim)
            return two_spins(real, imag)
        return two_spins(ahead_of(direction, real), ahead_of(direction, imag))

    def force(direction):
        outer_real = outer_imag = None
        for sign, field, index, other in ((-1, eta, 1, xi), (1, xi, 0, eta)):
            left_real, left_imag = half_ahead(direction, sign, field, index)
            right_real, right_imag = project(direction, sign, other)
            for s in range(2):
                lr, li = left_real[s][:, None], left_imag[s][:, None]
                rr, ri = right_real[s][None], right_imag[s][None]
                part_real = lr * rr + li * ri
                part_imag = li * rr - lr * ri
                outer_real = part_real if outer_real is None else outer_real + part_real
                outer_imag = part_imag if outer_imag is None else outer_imag + part_imag
        force_real = force_imag = None
        for c in range(3):
            mr, mi = gauge[direction, 0, :, c][:, None], gauge[direction, 1, :, c][:, None]
            orr, oi = outer_real[c][None], outer_imag[c][None]
            part_real = mr * orr - mi * oi
            part_imag = mr * oi + mi * orr
            force_real = part_real if c == 0 else force_real + part_real
            force_imag = part_imag if c == 0 else force_imag + part_imag
        half_step = 0.5 * step_size
        trace = (force_imag[0, 0] + force_imag[1, 1] + force_imag[2, 2]) * (step_size / 3.0)
        for a in range(3):
            updated[direction, 0, a, a] = momentum[direction, 0, a, a]
            updated[direction, 1, a, a] = momentum[direction, 1, a, a] - (
                step_size * force_imag[a, a] - trace
            )
            for b in range(a):
                anti = half_step * (force_real[a, b] - force_real[b, a])
                updated[direction, 0, a, b] = momentum[direction, 0, a, b] - anti
                updated[direction, 0, b, a] = momentum[direction, 0, b, a] + anti
                sym = half_step * (force_imag[a, b] + force_imag[b, a])
                updated[direction, 1, a, b] = momentum[direction, 1, a, b] - sym
                updated[direction, 1, b, a] = momentum[direction, 1, b, a] - sym

    store_updated = pltpu.make_async_copy(updated, updated_hbm, store_sem.at[0])
    store_solution = pltpu.make_async_copy(psi, solution_hbm, store_sem.at[1])

    loads[1].wait()
    out_row = lax.broadcasted_iota(jnp.int32, (LANES, LANES), 0)
    in_row = lax.broadcasted_iota(jnp.int32, (LANES, LANES), 1)
    place = (out_row // ROWS) * ROWS + (out_row % SLICE) * 2 + (out_row % ROWS) // SLICE
    permute = jnp.where(in_row == place, 1.0, 0.0).astype(jnp.bfloat16)
    blocks = LANES // ROWS
    for group in range(clover_low.shape[0] // LANES):
        moved = jnp.dot(
            permute, clover_low[group * LANES : (group + 1) * LANES], preferred_element_type=jnp.float32
        ).reshape(blocks, ROWS, LANES)
        for i in range(blocks):
            entry = group * blocks + i
            clover[entry // 72, entry // 36 % 2, entry // 6 % 6, entry % 6] = moved[i]
    loads[0].wait()
    clover_apply(read_total(source))
    loads[2].wait()
    for direction in range(4):
        for part in range(2):
            links[direction, part] = hop_scale * gauge[direction, part]
    pl.semaphore_wait(barrier, 4)
    send_halos(0)
    loads[3].wait()
    loads[4].wait()
    send_rims()
    loads[5].wait()

    def iteration(k, carry):
        slot = lax.rem(k - 1, 2)
        local_hops()

        @pl.when(k == 2)
        def _():
            for copy in rim_copies():
                copy.wait()
            for direction in range(4):
                force(direction)
            store_updated.start()

        clover_apply(receive_halos(slot))

        @pl.when(k < ITERS)
        def _():
            send_halos(lax.rem(k, 2))

        for copy in halo_copies(slot):
            copy.wait_send()
        return carry

    lax.fori_loop(1, ITERS + 1, iteration, 0)
    store_solution.start()
    store_updated.wait()
    store_solution.wait()


def per_device(gauge, clover_inverse, source, xi, eta, momentum):
    field = (2, 4, 3, ROWS, LANES)
    matrices = (4, 2, 3, 3, ROWS, LANES)
    half = (2, 3, 2 * ROWS, LANES)
    full = (2, 6, 2 * ROWS, LANES)
    chunks = LANES * SLICE // LANES
    low = clover_inverse.reshape(2, 2, 6, 6, 2, chunks, LANES)
    low = jnp.swapaxes(low, 4, 5).reshape(2 * 2 * 6 * 6 * chunks * 2, LANES)
    f32, bf16 = jnp.float32, jnp.bfloat16
    anywhere = pl.BlockSpec(memory_space=pl.ANY)
    solved, updated = pl.pallas_call(
        kernel,
        out_shape=(jax.ShapeDtypeStruct(field, f32), jax.ShapeDtypeStruct(matrices, f32)),
        in_specs=[anywhere] * 6,
        out_specs=(anywhere, anywhere),
        scratch_shapes=[
            pltpu.VMEM(matrices, f32),
            pltpu.VMEM(low.shape, bf16),
            pltpu.VMEM(field, f32),
            pltpu.VMEM(field, f32),
            pltpu.VMEM(field, f32),
            pltpu.VMEM(matrices, f32),
            pltpu.VMEM(matrices, f32),
            pltpu.VMEM((2, 2, 6, 6, ROWS, LANES), f32),
            pltpu.VMEM(field, f32),
            pltpu.VMEM(field, f32),
            pltpu.VMEM(matrices, f32),
            pltpu.VMEM((2, 6, ROWS, LANES), f32),
            pltpu.VMEM((2, 6, ROWS, LANES), f32),
            pltpu.VMEM(half, bf16),
            pltpu.VMEM(half, bf16),
            pltpu.VMEM(full, bf16),
            pltpu.VMEM(full, bf16),
            pltpu.VMEM(half, bf16),
            pltpu.VMEM(half, bf16),
            pltpu.VMEM(full, bf16),
            pltpu.VMEM(full, bf16),
            pltpu.VMEM((2, 6, ROWS, LANES), f32),
            pltpu.VMEM((2, 2, 6, ROWS, LANES), f32),
            pltpu.VMEM((2, 6, ROWS, LANES), f32),
            pltpu.VMEM((2, 2, 6, ROWS, LANES), f32),
            pltpu.SemaphoreType.DMA((6,)),
            pltpu.SemaphoreType.DMA((2,)),
            pltpu.SemaphoreType.DMA((4, 2)),
            pltpu.SemaphoreType.DMA((4, 2)),
            pltpu.SemaphoreType.DMA((2,)),
            pltpu.SemaphoreType.DMA((2,)),
        ],
        compiler_params=pltpu.CompilerParams(collective_id=0, has_side_effects=True),
        name="solve",
    )(
        gauge.reshape(matrices), low, source.reshape(field), xi.reshape(field),
        eta.reshape(field), momentum.reshape(matrices),
    )
    return solved.reshape(source.shape), updated.reshape(momentum.shape)


def solution(mesh):
    spinors = P(None, None, None, "ta", "xyz", None, None)
    matrices = P(None, None, None, None, "ta", "xyz", None, None)
    return jax.shard_map(
        per_device,
        mesh=mesh,
        in_specs=(matrices, matrices, spinors, spinors, spinors, matrices),
        out_specs=(spinors, matrices),
        check_vma=False,
    )
```

```python
import functools

import jax
import jax.numpy as jnp
from jax import lax
from jax.experimental import pallas as pl
from jax.experimental.pallas import tpu as pltpu
from jax.sharding import PartitionSpec as P

NZ = 64
ITERS = 8

hop_scale = 0.18
step_size = 0.25

ROWS = 8
LANES = 128
SLICE = 4


def combine(base, sign, term):
    return base + term if sign > 0 else base - term


def rotated(direction, sign, real, imag):
    if direction == 0:
        return [(sign, real[0]), (sign, real[1])], [(sign, imag[0]), (sign, imag[1])]
    if direction == 1:
        sig_real = [(1, real[1]), (1, real[0])]
        sig_imag = [(1, imag[1]), (1, imag[0])]
    elif direction == 2:
        sig_real = [(1, imag[1]), (-1, imag[0])]
        sig_imag = [(-1, real[1]), (1, real[0])]
    else:
        sig_real = [(1, real[0]), (-1, real[1])]
        sig_imag = [(1, imag[0]), (-1, imag[1])]
    return [(-sign * s, v) for s, v in sig_imag], [(sign * s, v) for s, v in sig_real]


def project(direction, sign, spinor):
    inverse_sign = sign if direction == 0 else -sign
    lower_real, lower_imag = rotated(
        direction, inverse_sign, [spinor[0, 2], spinor[0, 3]], [spinor[1, 2], spinor[1, 3]]
    )
    real = [combine(spinor[0, s], *lower_real[s]) for s in range(2)]
    imag = [combine(spinor[1, s], *lower_imag[s]) for s in range(2)]
    return real, imag


def add_expanded(total, direction, sign, half):
    real, imag = half
    lower_real, lower_imag = rotated(direction, sign, real, imag)
    new_real = [total[0][s] + real[s] for s in range(2)]
    new_real += [combine(total[0][2 + s], *lower_real[s]) for s in range(2)]
    new_imag = [total[1][s] + imag[s] for s in range(2)]
    new_imag += [combine(total[1][2 + s], *lower_imag[s]) for s in range(2)]
    return [new_real, new_imag]


def link_apply(links, direction, half):
    real, imag = half
    out_real, out_imag = [None, None], [None, None]
    for b in range(3):
        mat_real = links[direction, 0, :, b]
        mat_imag = links[direction, 1, :, b]
        for s in range(2):
            vec_real, vec_imag = real[s][b : b + 1], imag[s][b : b + 1]
            part_real = mat_real * vec_real - mat_imag * vec_imag
            part_imag = mat_real * vec_imag + mat_imag * vec_real
            out_real[s] = part_real if b == 0 else out_real[s] + part_real
            out_imag[s] = part_imag if b == 0 else out_imag[s] + part_imag
    return out_real, out_imag


def dagger_apply(links, direction, half):
    real, imag = half
    out_real, out_imag = [None, None], [None, None]
    for b in range(3):
        mat_real = links[direction, 0, b]
        mat_imag = links[direction, 1, b]
        for s in range(2):
            vec_real, vec_imag = real[s][b : b + 1], imag[s][b : b + 1]
            part_real = mat_real * vec_real + mat_imag * vec_imag
            part_imag = mat_real * vec_imag - mat_imag * vec_real
            out_real[s] = part_real if b == 0 else out_real[s] + part_real
            out_imag[s] = part_imag if b == 0 else out_imag[s] + part_imag
    return out_real, out_imag


def row_of(shape):
    return lax.broadcasted_iota(jnp.int32, shape, len(shape) - 2)


def lane_of(shape):
    return lax.broadcasted_iota(jnp.int32, shape, len(shape) - 1)


def roll(x, shift, axis):
    return pltpu.roll(x, shift, axis=x.ndim - 2 + axis)


def swap_slices(x):
    return roll(x, SLICE, 0)


def ahead_of(direction, x):
    if direction == 3:
        last = lane_of(x.shape) % NZ == NZ - 1
        return jnp.where(last, roll(x, NZ - 1, 1), roll(x, LANES - 1, 1))
    halves = roll(x, NZ, 1)
    row = row_of(x.shape) % SLICE
    next_pair = jnp.where(row == SLICE - 1, roll(halves, SLICE - 1, 0), roll(halves, ROWS - 1, 0))
    return jnp.where(lane_of(x.shape) < NZ, halves, next_pair)


def behind_of(direction, x):
    if direction == 3:
        first = lane_of(x.shape) % NZ == 0
        return jnp.where(first, roll(x, LANES - NZ + 1, 1), roll(x, 1, 1))
    halves = roll(x, NZ, 1)
    row = row_of(x.shape) % SLICE
    last_pair = jnp.where(row == 0, roll(halves, ROWS - SLICE + 1, 0), roll(halves, 1, 0))
    return jnp.where(lane_of(x.shape) < NZ, last_pair, halves)


def both_spins(half):
    return [jnp.concatenate(part, axis=0) for part in half]


def two_spins(real, imag):
    return [real[:3], real[3:]], [imag[:3], imag[3:]]


def to_bf16(x):
    return x.reshape(x.shape[0] // 2, 2 * ROWS, LANES).astype(jnp.bfloat16)


def to_f32(x):
    return x.astype(jnp.float32).reshape(2 * x.shape[0], ROWS, LANES)


def first_slice(real, imag):
    return jnp.where(row_of(real.shape) < SLICE, real, swap_slices(imag))


def last_slice(real, imag):
    return jnp.where(row_of(real.shape) < SLICE, swap_slices(real), imag)


def kernel(
    gauge_hbm, clover_hbm, source_hbm, xi_hbm, eta_hbm, momentum_hbm,
    psi, updated,
    gauge, clover_low, source, xi, eta, momentum,
    links, clover, total, t_ahead_local, t_behind_local,
    t_minus, t_plus, x_minus, x_plus,
    t_ahead, t_behind, x_ahead, x_behind,
    rim_t, rim_x, rim_t_ahead, rim_x_ahead,
    load_sem, send_sem, recv_sem, rim_send_sem, rim_recv_sem,
):
    n_t, n_x = lax.axis_size("ta"), lax.axis_size("xyz")
    my_t, my_x = lax.axis_index("ta"), lax.axis_index("xyz")
    t_next, t_last = {"ta": lax.rem(my_t + 1, n_t)}, {"ta": lax.rem(my_t + n_t - 1, n_t)}
    x_next, x_last = {"xyz": lax.rem(my_x + 1, n_x)}, {"xyz": lax.rem(my_x + n_x - 1, n_x)}

    barrier = pltpu.get_barrier_semaphore()
    for device in (t_next, t_last, x_next, x_last):
        pl.semaphore_signal(barrier, inc=1, device_id=device, device_id_type=pl.DeviceIdType.MESH)

    loads = [
        pltpu.make_async_copy(src, dst, load_sem.at[i])
        for i, (src, dst) in enumerate([
            (source_hbm, source), (clover_hbm, clover_low), (gauge_hbm, gauge),
            (xi_hbm, xi), (eta_hbm, eta), (momentum_hbm, momentum),
        ])
    ]
    for load in loads:
        load.start()

    def remote(src, dst, send, recv, device):
        return pltpu.make_async_remote_copy(
            src_ref=src, dst_ref=dst, send_sem=send, recv_sem=recv,
            device_id=device, device_id_type=pl.DeviceIdType.MESH,
        )

    def halo_copies(slot):
        return [
            remote(src.at[slot], dst.at[slot], send_sem.at[i, slot], recv_sem.at[i, slot], device)
            for i, (src, dst, device) in enumerate([
                (t_minus, t_ahead, t_last), (t_plus, t_behind, t_next),
                (x_minus, x_ahead, x_last), (x_plus, x_behind, x_next),
            ])
        ]

    def rim_copies():
        return [
            remote(rim_t, rim_t_ahead, rim_send_sem.at[0], rim_recv_sem.at[0], t_last),
            remote(rim_x, rim_x_ahead, rim_send_sem.at[1], rim_recv_sem.at[1], x_last),
        ]

    def clover_apply(vector):
        for chiral in range(2):
            out_real = out_imag = None
            for j in range(6):
                spin, colour = 2 * chiral + j // 3, j % 3
                vec_real = vector[0][spin][colour : colour + 1]
                vec_imag = vector[1][spin][colour : colour + 1]
                mat_real = clover[chiral, 0, :, j]
                mat_imag = clover[chiral, 1, :, j]
                part_real = mat_real * vec_real - mat_imag * vec_imag
                part_imag = mat_real * vec_imag + mat_imag * vec_real
                out_real = part_real if j == 0 else out_real + part_real
                out_imag = part_imag if j == 0 else out_imag + part_imag
            for s in range(2):
                psi[0, 2 * chiral + s] = out_real[3 * s : 3 * s + 3]
                psi[1, 2 * chiral + s] = out_imag[3 * s : 3 * s + 3]

    def send_halos(slot):
        copies = halo_copies(slot)
        real, imag = both_spins(project(0, -1, psi))
        t_minus[slot] = to_bf16(first_slice(real, imag))
        copies[0].start()
        t_ahead_local[0] = swap_slices(real)
        t_ahead_local[1] = swap_slices(imag)
        real, imag = both_spins(dagger_apply(links, 0, project(0, 1, psi)))
        t_plus[slot] = to_bf16(last_slice(real, imag))
        copies[1].start()
        t_behind_local[0] = swap_slices(real)
        t_behind_local[1] = swap_slices(imag)
        x_minus[slot] = to_bf16(jnp.concatenate(both_spins(project(1, -1, psi)), axis=0))
        copies[2].start()
        x_plus[slot] = to_bf16(
            jnp.concatenate(both_spins(dagger_apply(links, 1, project(1, 1, psi))), axis=0)
        )
        copies[3].start()

    def read_total(ref):
        return [[ref[part, s] for s in range(4)] for part in range(2)]

    def local_hops():
        result = read_total(source)
        for direction in (2, 3):
            half = both_spins(project(direction, -1, psi))
            half = two_spins(*[ahead_of(direction, part) for part in half])
            result = add_expanded(result, direction, -1, link_apply(links, direction, half))
            half = both_spins(dagger_apply(links, direction, project(direction, 1, psi)))
            half = two_spins(*[behind_of(direction, part) for part in half])
            result = add_expanded(result, direction, 1, half)
        for part in range(2):
            for s in range(4):
                total[part, s] = result[part][s]

    def receive_halos(slot):
        copies = halo_copies(slot)
        result = read_total(total)
        copies[2].wait_recv()
        half = to_f32(x_ahead[slot])
        result = add_expanded(result, 1, -1, link_apply(links, 1, two_spins(half[:6], half[6:])))
        copies[3].wait_recv()
        half = to_f32(x_behind[slot])
        result = add_expanded(result, 1, 1, two_spins(half[:6], half[6:]))
        copies[0].wait_recv()
        rim = to_f32(t_ahead[slot])
        first = row_of(rim.shape) < SLICE
        half = two_spins(
            jnp.where(first, t_ahead_local[0], swap_slices(rim)), jnp.where(first, t_ahead_local[1], rim)
        )
        result = add_expanded(result, 0, -1, link_apply(links, 0, half))
        copies[1].wait_recv()
        rim = to_f32(t_behind[slot])
        half = two_spins(
            jnp.where(first, rim, t_behind_local[0]), jnp.where(first, swap_slices(rim), t_behind_local[1])
        )
        return add_expanded(result, 0, 1, half)

    def send_rims():
        copies = rim_copies()
        for i, (sign, field) in enumerate([(1, xi), (-1, eta)]):
            real, imag = both_spins(project(0, sign, field))
            rim_t[i] = first_slice(real, imag)
            real, imag = both_spins(project(1, sign, field))
            rim_x[i, 0] = real
            rim_x[i, 1] = imag
        for copy in copies:
            copy.start()

    def half_ahead(direction, sign, field, index):
        if direction == 1:
            return two_spins(rim_x_ahead[index, 0], rim_x_ahead[index, 1])
        real, imag = both_spins(project(direction, sign, field))
        if direction == 0:
            rim = rim_t_ahead[index]
            first = row_of(rim.shape) < SLICE
            real = jnp.where(first, swap_slices(real), swap_slices(rim))
            imag = jnp.where(first, swap_slices(imag), rim)
            return two_spins(real, imag)
        return two_spins(ahead_of(direction, real), ahead_of(direction, imag))

    def force(direction):
        outer_real = outer_imag = None
        for sign, field, index, other in ((-1, eta, 1, xi), (1, xi, 0, eta)):
            left_real, left_imag = half_ahead(direction, sign, field, index)
            right_real, right_imag = project(direction, sign, other)
            for s in range(2):
                lr, li = left_real[s][:, None], left_imag[s][:, None]
                rr, ri = right_real[s][None], right_imag[s][None]
                part_real = lr * rr + li * ri
                part_imag = li * rr - lr * ri
                outer_real = part_real if outer_real is None else outer_real + part_real
                outer_imag = part_imag if outer_imag is None else outer_imag + part_imag
        force_real = force_imag = None
        for c in range(3):
            mr, mi = gauge[direction, 0, :, c][:, None], gauge[direction, 1, :, c][:, None]
            orr, oi = outer_real[c][None], outer_imag[c][None]
            part_real = mr * orr - mi * oi
            part_imag = mr * oi + mi * orr
            force_real = part_real if c == 0 else force_real + part_real
            force_imag = part_imag if c == 0 else force_imag + part_imag
        half_step = 0.5 * step_size
        trace = (force_imag[0, 0] + force_imag[1, 1] + force_imag[2, 2]) * (step_size / 3.0)
        for a in range(3):
            updated[direction, 0, a, a] = momentum[direction, 0, a, a]
            updated[direction, 1, a, a] = momentum[direction, 1, a, a] - (
                step_size * force_imag[a, a] - trace
            )
            for b in range(a):
                anti = half_step * (force_real[a, b] - force_real[b, a])
                updated[direction, 0, a, b] = momentum[direction, 0, a, b] - anti
                updated[direction, 0, b, a] = momentum[direction, 0, b, a] + anti
                sym = half_step * (force_imag[a, b] + force_imag[b, a])
                updated[direction, 1, a, b] = momentum[direction, 1, a, b] - sym
                updated[direction, 1, b, a] = momentum[direction, 1, b, a] - sym

    loads[1].wait()
    out_row = lax.broadcasted_iota(jnp.int32, (LANES, LANES), 0)
    in_row = lax.broadcasted_iota(jnp.int32, (LANES, LANES), 1)
    place = (out_row // ROWS) * ROWS + (out_row % SLICE) * 2 + (out_row % ROWS) // SLICE
    permute = jnp.where(in_row == place, 1.0, 0.0).astype(jnp.bfloat16)
    blocks = LANES // ROWS
    for group in range(clover_low.shape[0] // LANES):
        moved = jnp.dot(
            permute, clover_low[group * LANES : (group + 1) * LANES], preferred_element_type=jnp.float32
        ).reshape(blocks, ROWS, LANES)
        for i in range(blocks):
            entry = group * blocks + i
            clover[entry // 72, entry // 36 % 2, entry // 6 % 6, entry % 6] = moved[i]
    loads[0].wait()
    clover_apply(read_total(source))
    loads[2].wait()
    for direction in range(4):
        for part in range(2):
            links[direction, part] = hop_scale * gauge[direction, part]
    pl.semaphore_wait(barrier, 4)
    send_halos(0)
    loads[3].wait()
    loads[4].wait()
    send_rims()
    loads[5].wait()

    def iteration(k, carry):
        slot = lax.rem(k - 1, 2)
        local_hops()

        @pl.when(k == 2)
        def _():
            for copy in rim_copies():
                copy.wait()
            for direction in range(4):
                force(direction)

        clover_apply(receive_halos(slot))

        @pl.when(k < ITERS)
        def _():
            send_halos(lax.rem(k, 2))

        for copy in halo_copies(slot):
            copy.wait_send()
        return carry

    lax.fori_loop(1, ITERS + 1, iteration, 0)


def publish(solved, updated, solved_out, updated_out, sem):
    copies = [
        pltpu.make_async_copy(solved, solved_out, sem.at[0]),
        pltpu.make_async_copy(updated, updated_out, sem.at[1]),
    ]
    for copy in copies:
        copy.start()
    for copy in copies:
        copy.wait()


def per_device(gauge, clover_inverse, source, xi, eta, momentum):
    field = (2, 4, 3, ROWS, LANES)
    matrices = (4, 2, 3, 3, ROWS, LANES)
    half = (2, 3, 2 * ROWS, LANES)
    full = (2, 6, 2 * ROWS, LANES)
    chunks = LANES * SLICE // LANES
    low = clover_inverse.reshape(2, 2, 6, 6, 2, chunks, LANES)
    low = jnp.swapaxes(low, 4, 5).reshape(2 * 2 * 6 * 6 * chunks * 2, LANES)
    f32, bf16 = jnp.float32, jnp.bfloat16
    anywhere = pl.BlockSpec(memory_space=pl.ANY)
    in_hbm = pl.BlockSpec(memory_space=pltpu.HBM)
    on_chip = pl.BlockSpec(memory_space=pltpu.VMEM)
    solved, updated = pl.pallas_call(
        kernel,
        out_shape=(pltpu.VMEM(field, f32), pltpu.VMEM(matrices, f32)),
        in_specs=[anywhere] * 6,
        out_specs=(on_chip, on_chip),
        scratch_shapes=[
            pltpu.VMEM(matrices, f32),
            pltpu.VMEM(low.shape, bf16),
            pltpu.VMEM(field, f32),
            pltpu.VMEM(field, f32),
            pltpu.VMEM(field, f32),
            pltpu.VMEM(matrices, f32),
            pltpu.VMEM(matrices, f32),
            pltpu.VMEM((2, 2, 6, 6, ROWS, LANES), f32),
            pltpu.VMEM(field, f32),
            pltpu.VMEM((2, 6, ROWS, LANES), f32),
            pltpu.VMEM((2, 6, ROWS, LANES), f32),
            pltpu.VMEM(half, bf16),
            pltpu.VMEM(half, bf16),
            pltpu.VMEM(full, bf16),
            pltpu.VMEM(full, bf16),
            pltpu.VMEM(half, bf16),
            pltpu.VMEM(half, bf16),
            pltpu.VMEM(full, bf16),
            pltpu.VMEM(full, bf16),
            pltpu.VMEM((2, 6, ROWS, LANES), f32),
            pltpu.VMEM((2, 2, 6, ROWS, LANES), f32),
            pltpu.VMEM((2, 6, ROWS, LANES), f32),
            pltpu.VMEM((2, 2, 6, ROWS, LANES), f32),
            pltpu.SemaphoreType.DMA((6,)),
            pltpu.SemaphoreType.DMA((4, 2)),
            pltpu.SemaphoreType.DMA((4, 2)),
            pltpu.SemaphoreType.DMA((2,)),
            pltpu.SemaphoreType.DMA((2,)),
        ],
        compiler_params=pltpu.CompilerParams(collective_id=0, has_side_effects=True),
        name="solve",
    )(
        gauge.reshape(matrices), low, source.reshape(field), xi.reshape(field),
        eta.reshape(field), momentum.reshape(matrices),
    )
    solved, updated = pl.pallas_call(
        publish,
        out_shape=(jax.ShapeDtypeStruct(field, f32), jax.ShapeDtypeStruct(matrices, f32)),
        in_specs=[on_chip] * 2,
        out_specs=(in_hbm, in_hbm),
        scratch_shapes=[pltpu.SemaphoreType.DMA((2,))],
        compiler_params=pltpu.CompilerParams(vmem_limit_bytes=1 << 20),
        name="publish",
    )(solved, updated)
    return solved.reshape(source.shape), updated.reshape(momentum.shape)


def solution(mesh):
    spinors = P(None, None, None, "ta", "xyz", None, None)
    matrices = P(None, None, None, None, "ta", "xyz", None, None)
    return jax.shard_map(
        per_device,
        mesh=mesh,
        in_specs=(matrices, matrices, spinors, spinors, spinors, matrices),
        out_specs=(spinors, matrices),
        check_vma=False,
    )
```

```python
import functools

import jax
import jax.numpy as jnp
from jax import lax
from jax.experimental import pallas as pl
from jax.experimental.pallas import tpu as pltpu
from jax.sharding import PartitionSpec as P

NZ = 64
ITERS = 8

hop_scale = 0.18
step_size = 0.25

ROWS = 8
LANES = 128
SLICE = 4

SWITCH = 4
RIMS_AT = 4
FORCE_AT = 6


def combine(base, sign, term):
    return base + term if sign > 0 else base - term


def rotated(direction, sign, real, imag):
    if direction == 0:
        return [(sign, real[0]), (sign, real[1])], [(sign, imag[0]), (sign, imag[1])]
    if direction == 1:
        sig_real = [(1, real[1]), (1, real[0])]
        sig_imag = [(1, imag[1]), (1, imag[0])]
    elif direction == 2:
        sig_real = [(1, imag[1]), (-1, imag[0])]
        sig_imag = [(-1, real[1]), (1, real[0])]
    else:
        sig_real = [(1, real[0]), (-1, real[1])]
        sig_imag = [(1, imag[0]), (-1, imag[1])]
    return [(-sign * s, v) for s, v in sig_imag], [(sign * s, v) for s, v in sig_real]


def project(direction, sign, spinor):
    inverse_sign = sign if direction == 0 else -sign
    lower_real, lower_imag = rotated(
        direction, inverse_sign, [spinor[0, 2], spinor[0, 3]], [spinor[1, 2], spinor[1, 3]]
    )
    real = [combine(spinor[0, s], *lower_real[s]) for s in range(2)]
    imag = [combine(spinor[1, s], *lower_imag[s]) for s in range(2)]
    return real, imag


def add_expanded(total, direction, sign, half):
    real, imag = half
    lower_real, lower_imag = rotated(direction, sign, real, imag)
    new_real = [total[0][s] + real[s] for s in range(2)]
    new_real += [combine(total[0][2 + s], *lower_real[s]) for s in range(2)]
    new_imag = [total[1][s] + imag[s] for s in range(2)]
    new_imag += [combine(total[1][2 + s], *lower_imag[s]) for s in range(2)]
    return [new_real, new_imag]


def link_apply(links, direction, half):
    real, imag = half
    out_real, out_imag = [None, None], [None, None]
    for b in range(3):
        mat_real = links[direction, 0, :, b]
        mat_imag = links[direction, 1, :, b]
        for s in range(2):
            vec_real, vec_imag = real[s][b : b + 1], imag[s][b : b + 1]
            part_real = mat_real * vec_real - mat_imag * vec_imag
            part_imag = mat_real * vec_imag + mat_imag * vec_real
            out_real[s] = part_real if b == 0 else out_real[s] + part_real
            out_imag[s] = part_imag if b == 0 else out_imag[s] + part_imag
    return out_real, out_imag


def dagger_apply(links, direction, half):
    real, imag = half
    out_real, out_imag = [None, None], [None, None]
    for b in range(3):
        mat_real = links[direction, 0, b]
        mat_imag = links[direction, 1, b]
        for s in range(2):
            vec_real, vec_imag = real[s][b : b + 1], imag[s][b : b + 1]
            part_real = mat_real * vec_real + mat_imag * vec_imag
            part_imag = mat_real * vec_imag - mat_imag * vec_real
            out_real[s] = part_real if b == 0 else out_real[s] + part_real
            out_imag[s] = part_imag if b == 0 else out_imag[s] + part_imag
    return out_real, out_imag


def row_of(shape):
    return lax.broadcasted_iota(jnp.int32, shape, len(shape) - 2)


def lane_of(shape):
    return lax.broadcasted_iota(jnp.int32, shape, len(shape) - 1)


def roll(x, shift, axis):
    return pltpu.roll(x, shift, axis=x.ndim - 2 + axis)


def swap_slices(x):
    return roll(x, SLICE, 0)


def ahead_of(direction, x):
    if direction == 3:
        last = lane_of(x.shape) % NZ == NZ - 1
        return jnp.where(last, roll(x, NZ - 1, 1), roll(x, LANES - 1, 1))
    halves = roll(x, NZ, 1)
    row = row_of(x.shape) % SLICE
    next_pair = jnp.where(row == SLICE - 1, roll(halves, SLICE - 1, 0), roll(halves, ROWS - 1, 0))
    return jnp.where(lane_of(x.shape) < NZ, halves, next_pair)


def behind_of(direction, x):
    if direction == 3:
        first = lane_of(x.shape) % NZ == 0
        return jnp.where(first, roll(x, LANES - NZ + 1, 1), roll(x, 1, 1))
    halves = roll(x, NZ, 1)
    row = row_of(x.shape) % SLICE
    last_pair = jnp.where(row == 0, roll(halves, ROWS - SLICE + 1, 0), roll(halves, 1, 0))
    return jnp.where(lane_of(x.shape) < NZ, last_pair, halves)


def both_spins(half):
    return [jnp.concatenate(part, axis=0) for part in half]


def two_spins(real, imag):
    return [real[:3], real[3:]], [imag[:3], imag[3:]]


def to_bf16(x):
    return x.reshape(x.shape[0] // 2, 2 * ROWS, LANES).astype(jnp.bfloat16)


def to_f32(x):
    return x.astype(jnp.float32).reshape(2 * x.shape[0], ROWS, LANES)


def first_slice(real, imag):
    return jnp.where(row_of(real.shape) < SLICE, real, swap_slices(imag))


def last_slice(real, imag):
    return jnp.where(row_of(real.shape) < SLICE, swap_slices(real), imag)


def spread(first, last):
    top = row_of(first.shape) < SLICE
    return jnp.where(top, first, swap_slices(last)), jnp.where(top, swap_slices(first), last)


def masked(rows, part):
    return jnp.where(rows, part, 0.0)


def kernel(
    gauge_hbm, clover_hbm, source_hbm, xi_hbm, eta_hbm, momentum_hbm,
    psi, updated,
    gauge, clover_low, source, xi, eta, momentum,
    links, clover, total, t_ahead_local, t_behind_local,
    t_minus, t_plus, x_minus, x_plus,
    t_ahead, t_behind, x_ahead, x_behind,
    rim_t, rim_x, rim_t_ahead, rim_x_ahead,
    rest, rest_in, corner, corner_in, bulk_clover, bulk_clover_in, bulk_links, bulk_links_in,
    clover_rim, links_rim, psi_rim, halo,
    load_sem, send_sem, recv_sem, once_send_sem, once_recv_sem, ready,
):
    n_t, n_x = lax.axis_size("ta"), lax.axis_size("xyz")
    my_t, my_x = lax.axis_index("ta"), lax.axis_index("xyz")
    t_next, t_last = {"ta": lax.rem(my_t + 1, n_t)}, {"ta": lax.rem(my_t + n_t - 1, n_t)}
    x_next, x_last = {"xyz": lax.rem(my_x + 1, n_x)}, {"xyz": lax.rem(my_x + n_x - 1, n_x)}
    mesh_id = pl.DeviceIdType.MESH

    barrier = pltpu.get_barrier_semaphore()
    for device in (t_next, t_last, x_next, x_last):
        pl.semaphore_signal(barrier, inc=1, device_id=device, device_id_type=mesh_id)

    loads = [
        pltpu.make_async_copy(src, dst, load_sem.at[i])
        for i, (src, dst) in enumerate([
            (source_hbm, source), (clover_hbm, clover_low), (gauge_hbm, gauge),
            (xi_hbm, xi), (eta_hbm, eta), (momentum_hbm, momentum),
        ])
    ]
    for load in loads:
        load.start()

    def remote(src, dst, send, recv, device):
        return pltpu.make_async_remote_copy(
            src_ref=src, dst_ref=dst, send_sem=send, recv_sem=recv,
            device_id=device, device_id_type=mesh_id,
        )

    def slot_copy(index, slot, src, dst, device):
        return remote(src, dst, send_sem.at[index, slot], recv_sem.at[index, slot], device)

    def t_copies(slot):
        return [
            slot_copy(0, slot, t_minus.at[slot], t_ahead.at[slot], t_last),
            slot_copy(1, slot, t_plus.at[slot], t_behind.at[slot], t_next),
        ]

    def x_copies(slot):
        return [
            slot_copy(2, slot, x_minus.at[slot], x_ahead.at[slot], x_last),
            slot_copy(3, slot, x_plus.at[slot], x_behind.at[slot], x_next),
        ]

    def rest_copies(slot):
        return [
            slot_copy(4 + i, slot, rest.at[slot, i], rest_in.at[slot, i], device)
            for i, device in enumerate((t_last, t_next))
        ]

    def corner_copies(slot):
        devices = [{**t, **x} for t in (t_last, t_next) for x in (x_last, x_next)]
        return [
            slot_copy(6 + i, slot, corner.at[slot, i], corner_in.at[slot, i], device)
            for i, device in enumerate(devices)
        ]

    def once_copy(index, src, dst, device):
        return remote(src, dst, once_send_sem.at[index], once_recv_sem.at[index], device)

    def rim_copies():
        return [once_copy(0, rim_t, rim_t_ahead, t_last), once_copy(1, rim_x, rim_x_ahead, x_last)]

    def bulk_copies():
        copies = []
        for i, device in enumerate((t_last, t_next)):
            copies.append(once_copy(2 + i, bulk_clover.at[i], bulk_clover_in.at[i], device))
            copies.append(once_copy(4 + i, bulk_links.at[i], bulk_links_in.at[i], device))
        return copies

    def clover_apply(blocks, vector, out):
        for chiral in range(2):
            out_real = out_imag = None
            for j in range(6):
                spin, colour = 2 * chiral + j // 3, j % 3
                vec_real = vector[0][spin][colour : colour + 1]
                vec_imag = vector[1][spin][colour : colour + 1]
                mat_real = blocks[chiral, 0, :, j]
                mat_imag = blocks[chiral, 1, :, j]
                part_real = mat_real * vec_real - mat_imag * vec_imag
                part_imag = mat_real * vec_imag + mat_imag * vec_real
                out_real = part_real if j == 0 else out_real + part_real
                out_imag = part_imag if j == 0 else out_imag + part_imag
            for s in range(2):
                out[0, 2 * chiral + s] = out_real[3 * s : 3 * s + 3]
                out[1, 2 * chiral + s] = out_imag[3 * s : 3 * s + 3]

    def send_halos(j):
        kept = lax.rem(j, 2)
        real, imag = both_spins(project(0, -1, psi))
        t_ahead_local[kept, 0] = swap_slices(real)
        t_ahead_local[kept, 1] = swap_slices(imag)
        real, imag = both_spins(dagger_apply(links, 0, project(0, 1, psi)))
        t_behind_local[kept, 0] = swap_slices(real)
        t_behind_local[kept, 1] = swap_slices(imag)

        @pl.when(j < SWITCH - 1)
        def _():
            copies = t_copies(j)
            top = row_of((6, ROWS, LANES)) < SLICE
            t_minus[j] = to_bf16(
                jnp.where(top, swap_slices(t_ahead_local[kept, 0]), t_ahead_local[kept, 1])
            )
            copies[0].start()
            t_plus[j] = to_bf16(
                jnp.where(top, t_behind_local[kept, 0], swap_slices(t_behind_local[kept, 1]))
            )
            copies[1].start()

        copies = x_copies(j)
        x_minus[j] = to_bf16(jnp.concatenate(both_spins(project(1, -1, psi)), axis=0))
        copies[0].start()
        x_plus[j] = to_bf16(
            jnp.concatenate(both_spins(dagger_apply(links, 1, project(1, 1, psi))), axis=0)
        )
        copies[1].start()

        @pl.when((j >= SWITCH - 2) & (j < ITERS - 1))
        def _():
            copies = corner_copies(j)
            for i, sent in enumerate((x_minus, x_plus)):
                value = to_f32(sent[j])
                corner[j, i] = to_bf16(first_slice(value[:6], value[6:]))
                copies[i].start()
                corner[j, 2 + i] = to_bf16(last_slice(value[:6], value[6:]))
                copies[2 + i].start()

    def read_total(ref):
        return [[ref[part, s] for s in range(4)] for part in range(2)]

    def write_total(ref, result):
        for part in range(2):
            for s in range(4):
                ref[part, s] = result[part][s]

    def local_hops(kept):
        result = read_total(source)
        for direction in (2, 3):
            half = both_spins(project(direction, -1, psi))
            half = two_spins(*[ahead_of(direction, part) for part in half])
            result = add_expanded(result, direction, -1, link_apply(links, direction, half))
            half = both_spins(dagger_apply(links, direction, project(direction, 1, psi)))
            half = two_spins(*[behind_of(direction, part) for part in half])
            result = add_expanded(result, direction, 1, half)
        top = row_of((6, ROWS, LANES)) < SLICE
        half = two_spins(*[masked(top, t_ahead_local[kept, part]) for part in range(2)])
        result = add_expanded(result, 0, -1, link_apply(links, 0, half))
        half = two_spins(*[masked(~top, t_behind_local[kept, part]) for part in range(2)])
        write_total(total, add_expanded(result, 0, 1, half))

    def send_rest(k):
        copies = rest_copies(k)
        real, imag = [jnp.concatenate(part, axis=0) for part in read_total(total)]
        rest[k, 0] = to_bf16(first_slice(real, imag))
        copies[0].start()
        rest[k, 1] = to_bf16(last_slice(real, imag))
        copies[1].start()

    def receive_bulk():
        for copy in bulk_copies():
            copy.wait_recv()
        for chiral in range(2):
            real, imag = spread(to_f32(bulk_clover_in[0, chiral]), to_f32(bulk_clover_in[1, chiral]))
            clover_rim[chiral, 0] = real.reshape(6, 6, ROWS, LANES)
            clover_rim[chiral, 1] = imag.reshape(6, 6, ROWS, LANES)
        real, imag = spread(to_f32(bulk_links_in[0]), to_f32(bulk_links_in[1]))
        for direction in range(2):
            links_rim[direction, 0] = real[9 * direction : 9 * direction + 9].reshape(3, 3, ROWS, LANES)
            links_rim[direction, 1] = imag[9 * direction : 9 * direction + 9].reshape(3, 3, ROWS, LANES)

    def receive_t(j):
        copies = t_copies(j)
        top = row_of((6, ROWS, LANES)) < SLICE
        copies[0].wait_recv()
        rim = to_f32(t_ahead[j])
        halo[0, 0] = masked(~top, swap_slices(rim))
        halo[0, 1] = masked(~top, rim)
        copies[1].wait_recv()
        rim = to_f32(t_behind[j])
        halo[1, 0] = masked(top, rim)
        halo[1, 1] = masked(top, swap_slices(rim))

    def iterate_rim(k):
        kept = lax.rem(k - 1, 2)
        top = row_of((6, ROWS, LANES)) < SLICE
        zero = jnp.zeros((3, ROWS, LANES), jnp.float32)
        result = [[zero] * 4, [zero] * 4]
        half = two_spins(*[masked(top, t_behind_local[kept, part]) for part in range(2)])
        result = add_expanded(result, 0, 1, half)
        half = two_spins(*[masked(~top, t_ahead_local[kept, part]) for part in range(2)])
        result = add_expanded(result, 0, -1, link_apply(links_rim, 0, half))
        for copy in rest_copies(k):
            copy.wait_recv()
        parts = spread(to_f32(rest_in[k, 0]), to_f32(rest_in[k, 1]))
        result = [
            [result[part][s] + parts[part][3 * s : 3 * s + 3] for s in range(4)] for part in range(2)
        ]
        for copy in corner_copies(k - 1):
            copy.wait_recv()
        half = two_spins(*spread(to_f32(corner_in[k - 1, 0]), to_f32(corner_in[k - 1, 2])))
        result = add_expanded(result, 1, -1, link_apply(links_rim, 1, half))
        half = two_spins(*spread(to_f32(corner_in[k - 1, 1]), to_f32(corner_in[k - 1, 3])))
        clover_apply(clover_rim, add_expanded(result, 1, 1, half), psi_rim)
        for part, value in enumerate(both_spins(project(0, -1, psi_rim))):
            halo[0, part] = masked(~top, swap_slices(value))
        for part, value in enumerate(both_spins(dagger_apply(links_rim, 0, project(0, 1, psi_rim)))):
            halo[1, part] = masked(top, swap_slices(value))

    def with_halos(slot):
        copies = x_copies(slot)
        result = read_total(total)
        half = two_spins(halo[0, 0], halo[0, 1])
        result = add_expanded(result, 0, -1, link_apply(links, 0, half))
        result = add_expanded(result, 0, 1, two_spins(halo[1, 0], halo[1, 1]))
        copies[0].wait_recv()
        half = to_f32(x_ahead[slot])
        result = add_expanded(result, 1, -1, link_apply(links, 1, two_spins(half[:6], half[6:])))
        copies[1].wait_recv()
        half = to_f32(x_behind[slot])
        return add_expanded(result, 1, 1, two_spins(half[:6], half[6:]))

    def send_bulk():
        for chiral in range(2):
            real = clover[chiral, 0].reshape(36, ROWS, LANES)
            imag = clover[chiral, 1].reshape(36, ROWS, LANES)
            bulk_clover[0, chiral] = to_bf16(first_slice(real, imag))
            bulk_clover[1, chiral] = to_bf16(last_slice(real, imag))
        real, imag = [
            jnp.concatenate([links[d, part].reshape(9, ROWS, LANES) for d in range(2)], axis=0)
            for part in range(2)
        ]
        bulk_links[0] = to_bf16(first_slice(real, imag))
        bulk_links[1] = to_bf16(last_slice(real, imag))
        for copy in bulk_copies():
            copy.start()

    def send_rims():
        copies = rim_copies()
        for i, (sign, field) in enumerate([(1, xi), (-1, eta)]):
            real, imag = both_spins(project(0, sign, field))
            rim_t[i] = first_slice(real, imag)
            real, imag = both_spins(project(1, sign, field))
            rim_x[i, 0] = real
            rim_x[i, 1] = imag
        for copy in copies:
            copy.start()

    def half_ahead(direction, sign, field, index):
        if direction == 1:
            return two_spins(rim_x_ahead[index, 0], rim_x_ahead[index, 1])
        real, imag = both_spins(project(direction, sign, field))
        if direction == 0:
            rim = rim_t_ahead[index]
            first = row_of(rim.shape) < SLICE
            real = jnp.where(first, swap_slices(real), swap_slices(rim))
            imag = jnp.where(first, swap_slices(imag), rim)
            return two_spins(real, imag)
        return two_spins(ahead_of(direction, real), ahead_of(direction, imag))

    def force(direction):
        outer_real = outer_imag = None
        for sign, field, index, other in ((-1, eta, 1, xi), (1, xi, 0, eta)):
            left_real, left_imag = half_ahead(direction, sign, field, index)
            right_real, right_imag = project(direction, sign, other)
            for s in range(2):
                lr, li = left_real[s][:, None], left_imag[s][:, None]
                rr, ri = right_real[s][None], right_imag[s][None]
                part_real = lr * rr + li * ri
                part_imag = li * rr - lr * ri
                outer_real = part_real if outer_real is None else outer_real + part_real
                outer_imag = part_imag if outer_imag is None else outer_imag + part_imag
        force_real = force_imag = None
        for c in range(3):
            mr, mi = gauge[direction, 0, :, c][:, None], gauge[direction, 1, :, c][:, None]
            orr, oi = outer_real[c][None], outer_imag[c][None]
            part_real = mr * orr - mi * oi
            part_imag = mr * oi + mi * orr
            force_real = part_real if c == 0 else force_real + part_real
            force_imag = part_imag if c == 0 else force_imag + part_imag
        half_step = 0.5 * step_size
        trace = (force_imag[0, 0] + force_imag[1, 1] + force_imag[2, 2]) * (step_size / 3.0)
        for a in range(3):
            updated[direction, 0, a, a] = momentum[direction, 0, a, a]
            updated[direction, 1, a, a] = momentum[direction, 1, a, a] - (
                step_size * force_imag[a, a] - trace
            )
            for b in range(a):
                anti = half_step * (force_real[a, b] - force_real[b, a])
                updated[direction, 0, a, b] = momentum[direction, 0, a, b] - anti
                updated[direction, 0, b, a] = momentum[direction, 0, b, a] + anti
                sym = half_step * (force_imag[a, b] + force_imag[b, a])
                updated[direction, 1, a, b] = momentum[direction, 1, a, b] - sym
                updated[direction, 1, b, a] = momentum[direction, 1, b, a] - sym

    loads[1].wait()
    out_row = lax.broadcasted_iota(jnp.int32, (LANES, LANES), 0)
    in_row = lax.broadcasted_iota(jnp.int32, (LANES, LANES), 1)
    place = (out_row // ROWS) * ROWS + (out_row % SLICE) * 2 + (out_row % ROWS) // SLICE
    permute = jnp.where(in_row == place, 1.0, 0.0).astype(jnp.bfloat16)
    blocks = LANES // ROWS
    for group in range(clover_low.shape[0] // LANES):
        moved = jnp.dot(
            permute, clover_low[group * LANES : (group + 1) * LANES], preferred_element_type=jnp.float32
        ).reshape(blocks, ROWS, LANES)
        for i in range(blocks):
            entry = group * blocks + i
            clover[entry // 72, entry // 36 % 2, entry // 6 % 6, entry % 6] = moved[i]
    loads[0].wait()
    clover_apply(clover, read_total(source), psi)
    loads[2].wait()
    for direction in range(4):
        for part in range(2):
            links[direction, part] = hop_scale * gauge[direction, part]
    pl.semaphore_wait(barrier, 4)
    send_halos(0)
    for device in (x_next, x_last):
        pl.semaphore_signal(ready, inc=1, device_id=device, device_id_type=mesh_id)
    send_bulk()
    for load in loads[3:]:
        load.wait()
    pl.semaphore_wait(ready, 2)

    def iteration(k, carry):
        local_hops(lax.rem(k - 1, 2))

        @pl.when((k >= SWITCH - 1) & (k < ITERS))
        def _():
            send_rest(k)

        @pl.when(k == RIMS_AT)
        def _():
            send_rims()

        @pl.when(k == FORCE_AT)
        def _():
            for copy in rim_copies():
                copy.wait()
            for direction in range(4):
                force(direction)

        @pl.when(k < SWITCH)
        def _():
            receive_t(k - 1)

        @pl.when(k == SWITCH)
        def _():
            receive_bulk()

        @pl.when(k >= SWITCH)
        def _():
            iterate_rim(k - 1)

        clover_apply(clover, with_halos(k - 1), psi)

        @pl.when(k < ITERS)
        def _():
            send_halos(k)

        return carry

    lax.fori_loop(1, ITERS + 1, iteration, 0)
    sent = bulk_copies()
    for j in range(ITERS):
        sent += x_copies(j)
        sent += t_copies(j) if j < SWITCH - 1 else []
        sent += corner_copies(j) if SWITCH - 2 <= j < ITERS - 1 else []
        sent += rest_copies(j) if j >= SWITCH - 1 else []
    for copy in sent:
        copy.wait_send()


def publish(solved, updated, solved_out, updated_out, sem):
    copies = [
        pltpu.make_async_copy(solved, solved_out, sem.at[0]),
        pltpu.make_async_copy(updated, updated_out, sem.at[1]),
    ]
    for copy in copies:
        copy.start()
    for copy in copies:
        copy.wait()


def per_device(gauge, clover_inverse, source, xi, eta, momentum):
    field = (2, 4, 3, ROWS, LANES)
    matrices = (4, 2, 3, 3, ROWS, LANES)
    half = (3, 2 * ROWS, LANES)
    full = (6, 2 * ROWS, LANES)
    chunks = LANES * SLICE // LANES
    low = clover_inverse.reshape(2, 2, 6, 6, 2, chunks, LANES)
    low = jnp.swapaxes(low, 4, 5).reshape(2 * 2 * 6 * 6 * chunks * 2, LANES)
    f32, bf16 = jnp.float32, jnp.bfloat16
    anywhere = pl.BlockSpec(memory_space=pl.ANY)
    in_hbm = pl.BlockSpec(memory_space=pltpu.HBM)
    on_chip = pl.BlockSpec(memory_space=pltpu.VMEM)
    solved, updated = pl.pallas_call(
        kernel,
        out_shape=(pltpu.VMEM(field, f32), pltpu.VMEM(matrices, f32)),
        in_specs=[anywhere] * 6,
        out_specs=(on_chip, on_chip),
        scratch_shapes=[
            pltpu.VMEM(matrices, f32),
            pltpu.VMEM(low.shape, bf16),
            pltpu.VMEM(field, f32),
            pltpu.VMEM(field, f32),
            pltpu.VMEM(field, f32),
            pltpu.VMEM(matrices, f32),
            pltpu.VMEM(matrices, f32),
            pltpu.VMEM((2, 2, 6, 6, ROWS, LANES), f32),
            pltpu.VMEM(field, f32),
            pltpu.VMEM((2, 2, 6, ROWS, LANES), f32),
            pltpu.VMEM((2, 2, 6, ROWS, LANES), f32),
            pltpu.VMEM((SWITCH - 1, *half), bf16),
            pltpu.VMEM((SWITCH - 1, *half), bf16),
            pltpu.VMEM((ITERS, *full), bf16),
            pltpu.VMEM((ITERS, *full), bf16),
            pltpu.VMEM((SWITCH - 1, *half), bf16),
            pltpu.VMEM((SWITCH - 1, *half), bf16),
            pltpu.VMEM((ITERS, *full), bf16),
            pltpu.VMEM((ITERS, *full), bf16),
            pltpu.VMEM((2, 6, ROWS, LANES), f32),
            pltpu.VMEM((2, 2, 6, ROWS, LANES), f32),
            pltpu.VMEM((2, 6, ROWS, LANES), f32),
            pltpu.VMEM((2, 2, 6, ROWS, LANES), f32),
            pltpu.VMEM((ITERS, 2, *full), bf16),
            pltpu.VMEM((ITERS, 2, *full), bf16),
            pltpu.VMEM((ITERS, 4, *half), bf16),
            pltpu.VMEM((ITERS, 4, *half), bf16),
            pltpu.VMEM((2, 2, 18, 2 * ROWS, LANES), bf16),
            pltpu.VMEM((2, 2, 18, 2 * ROWS, LANES), bf16),
            pltpu.VMEM((2, 9, 2 * ROWS, LANES), bf16),
            pltpu.VMEM((2, 9, 2 * ROWS, LANES), bf16),
            pltpu.VMEM((2, 2, 6, 6, ROWS, LANES), f32),
            pltpu.VMEM((2, 2, 3, 3, ROWS, LANES), f32),
            pltpu.VMEM(field, f32),
            pltpu.VMEM((2, 2, 6, ROWS, LANES), f32),
            pltpu.SemaphoreType.DMA((6,)),
            pltpu.SemaphoreType.DMA((10, ITERS)),
            pltpu.SemaphoreType.DMA((10, ITERS)),
            pltpu.SemaphoreType.DMA((6,)),
            pltpu.SemaphoreType.DMA((6,)),
            pltpu.SemaphoreType.REGULAR,
        ],
        compiler_params=pltpu.CompilerParams(collective_id=0, has_side_effects=True),
        name="solve",
    )(
        gauge.reshape(matrices), low, source.reshape(field), xi.reshape(field),
        eta.reshape(field), momentum.reshape(matrices),
    )
    solved, updated = pl.pallas_call(
        publish,
        out_shape=(jax.ShapeDtypeStruct(field, f32), jax.ShapeDtypeStruct(matrices, f32)),
        in_specs=[on_chip] * 2,
        out_specs=(in_hbm, in_hbm),
        scratch_shapes=[pltpu.SemaphoreType.DMA((2,))],
        compiler_params=pltpu.CompilerParams(vmem_limit_bytes=1 << 20),
        name="publish",
    )(solved, updated)
    return solved.reshape(source.shape), updated.reshape(momentum.shape)


def solution(mesh):
    spinors = P(None, None, None, "ta", "xyz", None, None)
    matrices = P(None, None, None, None, "ta", "xyz", None, None)
    return jax.shard_map(
        per_device,
        mesh=mesh,
        in_specs=(matrices, matrices, spinors, spinors, spinors, matrices),
        out_specs=(spinors, matrices),
        check_vma=False,
    )
```

```python
import functools

import jax
import jax.numpy as jnp
from jax import lax
from jax.experimental import pallas as pl
from jax.experimental.pallas import tpu as pltpu
from jax.sharding import PartitionSpec as P

NZ = 64
ITERS = 8

hop_scale = 0.18
step_size = 0.25

ROWS = 8
LANES = 128
SLICE = 4

SWITCH = 3
RIMS_AT = 4
FORCE_AT = 6


def combine(base, sign, term):
    return base + term if sign > 0 else base - term


def rotated(direction, sign, real, imag):
    if direction == 0:
        return [(sign, real[0]), (sign, real[1])], [(sign, imag[0]), (sign, imag[1])]
    if direction == 1:
        sig_real = [(1, real[1]), (1, real[0])]
        sig_imag = [(1, imag[1]), (1, imag[0])]
    elif direction == 2:
        sig_real = [(1, imag[1]), (-1, imag[0])]
        sig_imag = [(-1, real[1]), (1, real[0])]
    else:
        sig_real = [(1, real[0]), (-1, real[1])]
        sig_imag = [(1, imag[0]), (-1, imag[1])]
    return [(-sign * s, v) for s, v in sig_imag], [(sign * s, v) for s, v in sig_real]


def project(direction, sign, spinor):
    inverse_sign = sign if direction == 0 else -sign
    lower_real, lower_imag = rotated(
        direction, inverse_sign, [spinor[0, 2], spinor[0, 3]], [spinor[1, 2], spinor[1, 3]]
    )
    real = [combine(spinor[0, s], *lower_real[s]) for s in range(2)]
    imag = [combine(spinor[1, s], *lower_imag[s]) for s in range(2)]
    return real, imag


def add_expanded(total, direction, sign, half):
    real, imag = half
    lower_real, lower_imag = rotated(direction, sign, real, imag)
    new_real = [total[0][s] + real[s] for s in range(2)]
    new_real += [combine(total[0][2 + s], *lower_real[s]) for s in range(2)]
    new_imag = [total[1][s] + imag[s] for s in range(2)]
    new_imag += [combine(total[1][2 + s], *lower_imag[s]) for s in range(2)]
    return [new_real, new_imag]


def link_apply(links, direction, half):
    real, imag = half
    out_real, out_imag = [None, None], [None, None]
    for b in range(3):
        mat_real = links[direction, 0, :, b]
        mat_imag = links[direction, 1, :, b]
        for s in range(2):
            vec_real, vec_imag = real[s][b : b + 1], imag[s][b : b + 1]
            part_real = mat_real * vec_real - mat_imag * vec_imag
            part_imag = mat_real * vec_imag + mat_imag * vec_real
            out_real[s] = part_real if b == 0 else out_real[s] + part_real
            out_imag[s] = part_imag if b == 0 else out_imag[s] + part_imag
    return out_real, out_imag


def dagger_apply(links, direction, half):
    real, imag = half
    out_real, out_imag = [None, None], [None, None]
    for b in range(3):
        mat_real = links[direction, 0, b]
        mat_imag = links[direction, 1, b]
        for s in range(2):
            vec_real, vec_imag = real[s][b : b + 1], imag[s][b : b + 1]
            part_real = mat_real * vec_real + mat_imag * vec_imag
            part_imag = mat_real * vec_imag - mat_imag * vec_real
            out_real[s] = part_real if b == 0 else out_real[s] + part_real
            out_imag[s] = part_imag if b == 0 else out_imag[s] + part_imag
    return out_real, out_imag


def row_of(shape):
    return lax.broadcasted_iota(jnp.int32, shape, len(shape) - 2)


def lane_of(shape):
    return lax.broadcasted_iota(jnp.int32, shape, len(shape) - 1)


def roll(x, shift, axis):
    return pltpu.roll(x, shift, axis=x.ndim - 2 + axis)


def swap_slices(x):
    return roll(x, SLICE, 0)


def ahead_of(direction, x):
    if direction == 3:
        last = lane_of(x.shape) % NZ == NZ - 1
        return jnp.where(last, roll(x, NZ - 1, 1), roll(x, LANES - 1, 1))
    halves = roll(x, NZ, 1)
    row = row_of(x.shape) % SLICE
    next_pair = jnp.where(row == SLICE - 1, roll(halves, SLICE - 1, 0), roll(halves, ROWS - 1, 0))
    return jnp.where(lane_of(x.shape) < NZ, halves, next_pair)


def behind_of(direction, x):
    if direction == 3:
        first = lane_of(x.shape) % NZ == 0
        return jnp.where(first, roll(x, LANES - NZ + 1, 1), roll(x, 1, 1))
    halves = roll(x, NZ, 1)
    row = row_of(x.shape) % SLICE
    last_pair = jnp.where(row == 0, roll(halves, ROWS - SLICE + 1, 0), roll(halves, 1, 0))
    return jnp.where(lane_of(x.shape) < NZ, last_pair, halves)


def both_spins(half):
    return [jnp.concatenate(part, axis=0) for part in half]


def two_spins(real, imag):
    return [real[:3], real[3:]], [imag[:3], imag[3:]]


def to_bf16(x):
    return x.reshape(x.shape[0] // 2, 2 * ROWS, LANES).astype(jnp.bfloat16)


def to_f32(x):
    return x.astype(jnp.float32).reshape(2 * x.shape[0], ROWS, LANES)


def first_slice(real, imag):
    return jnp.where(row_of(real.shape) < SLICE, real, swap_slices(imag))


def last_slice(real, imag):
    return jnp.where(row_of(real.shape) < SLICE, swap_slices(real), imag)


def spread(first, last):
    top = row_of(first.shape) < SLICE
    return jnp.where(top, first, swap_slices(last)), jnp.where(top, swap_slices(first), last)


def masked(rows, part):
    return jnp.where(rows, part, 0.0)


def kernel(
    gauge_hbm, clover_hbm, source_hbm, xi_hbm, eta_hbm, momentum_hbm,
    psi, updated,
    gauge, clover_low, source, xi, eta, momentum,
    links, clover, total, t_ahead_local, t_behind_local,
    t_minus, t_plus, x_minus, x_plus,
    t_ahead, t_behind, x_ahead, x_behind,
    rim_t, rim_x, rim_t_ahead, rim_x_ahead,
    rest, rest_in, corner, corner_in, bulk_clover, bulk_clover_in, bulk_links, bulk_links_in,
    clover_rim, links_rim, psi_rim, halo,
    load_sem, send_sem, recv_sem, once_send_sem, once_recv_sem, ready,
):
    n_t, n_x = lax.axis_size("ta"), lax.axis_size("xyz")
    my_t, my_x = lax.axis_index("ta"), lax.axis_index("xyz")
    t_next, t_last = {"ta": lax.rem(my_t + 1, n_t)}, {"ta": lax.rem(my_t + n_t - 1, n_t)}
    x_next, x_last = {"xyz": lax.rem(my_x + 1, n_x)}, {"xyz": lax.rem(my_x + n_x - 1, n_x)}
    mesh_id = pl.DeviceIdType.MESH

    barrier = pltpu.get_barrier_semaphore()
    for device in (t_next, t_last, x_next, x_last):
        pl.semaphore_signal(barrier, inc=1, device_id=device, device_id_type=mesh_id)

    loads = [
        pltpu.make_async_copy(src, dst, load_sem.at[i])
        for i, (src, dst) in enumerate([
            (source_hbm, source), (clover_hbm, clover_low), (gauge_hbm, gauge),
            (xi_hbm, xi), (eta_hbm, eta), (momentum_hbm, momentum),
        ])
    ]
    for load in loads:
        load.start()

    def remote(src, dst, send, recv, device):
        return pltpu.make_async_remote_copy(
            src_ref=src, dst_ref=dst, send_sem=send, recv_sem=recv,
            device_id=device, device_id_type=mesh_id,
        )

    def slot_copy(index, slot, src, dst, device):
        return remote(src, dst, send_sem.at[index, slot], recv_sem.at[index, slot], device)

    def t_copies(slot):
        return [
            slot_copy(0, slot, t_minus.at[slot], t_ahead.at[slot], t_last),
            slot_copy(1, slot, t_plus.at[slot], t_behind.at[slot], t_next),
        ]

    def x_copies(slot):
        return [
            slot_copy(2, slot, x_minus.at[slot], x_ahead.at[slot], x_last),
            slot_copy(3, slot, x_plus.at[slot], x_behind.at[slot], x_next),
        ]

    def rest_copies(slot):
        return [
            slot_copy(4 + i, slot, rest.at[slot, i], rest_in.at[slot, i], device)
            for i, device in enumerate((t_last, t_next))
        ]

    def corner_copies(slot):
        devices = [{**t, **x} for t in (t_last, t_next) for x in (x_last, x_next)]
        return [
            slot_copy(6 + i, slot, corner.at[slot, i], corner_in.at[slot, i], device)
            for i, device in enumerate(devices)
        ]

    def once_copy(index, src, dst, device):
        return remote(src, dst, once_send_sem.at[index], once_recv_sem.at[index], device)

    def rim_copies():
        return [once_copy(0, rim_t, rim_t_ahead, t_last), once_copy(1, rim_x, rim_x_ahead, x_last)]

    def bulk_copies():
        copies = []
        for i, device in enumerate((t_last, t_next)):
            copies.append(once_copy(2 + i, bulk_clover.at[i, 0], bulk_clover_in.at[i, 0], device))
        for i, device in enumerate((t_last, t_next)):
            copies.append(once_copy(6 + i, bulk_clover.at[i, 1], bulk_clover_in.at[i, 1], device))
            copies.append(once_copy(4 + i, bulk_links.at[i], bulk_links_in.at[i], device))
        return copies

    def clover_apply(blocks, vector, out):
        for chiral in range(2):
            out_real = out_imag = None
            for j in range(6):
                spin, colour = 2 * chiral + j // 3, j % 3
                vec_real = vector[0][spin][colour : colour + 1]
                vec_imag = vector[1][spin][colour : colour + 1]
                mat_real = blocks[chiral, 0, :, j]
                mat_imag = blocks[chiral, 1, :, j]
                part_real = mat_real * vec_real - mat_imag * vec_imag
                part_imag = mat_real * vec_imag + mat_imag * vec_real
                out_real = part_real if j == 0 else out_real + part_real
                out_imag = part_imag if j == 0 else out_imag + part_imag
            for s in range(2):
                out[0, 2 * chiral + s] = out_real[3 * s : 3 * s + 3]
                out[1, 2 * chiral + s] = out_imag[3 * s : 3 * s + 3]

    def send_x(j):
        copies = x_copies(j)
        x_minus[j] = to_bf16(jnp.concatenate(both_spins(project(1, -1, psi)), axis=0))
        copies[0].start()
        x_plus[j] = to_bf16(
            jnp.concatenate(both_spins(dagger_apply(links, 1, project(1, 1, psi))), axis=0)
        )
        copies[1].start()

    def keep_t(j):
        kept = lax.rem(j, 2)
        real, imag = both_spins(project(0, -1, psi))
        t_ahead_local[kept, 0] = swap_slices(real)
        t_ahead_local[kept, 1] = swap_slices(imag)
        real, imag = both_spins(dagger_apply(links, 0, project(0, 1, psi)))
        t_behind_local[kept, 0] = swap_slices(real)
        t_behind_local[kept, 1] = swap_slices(imag)

    def send_t(j):
        kept = lax.rem(j, 2)
        copies = t_copies(j)
        real, imag = both_spins(project(0, -1, psi))
        t_minus[j] = to_bf16(first_slice(real, imag))
        copies[0].start()
        t_ahead_local[kept, 0] = swap_slices(real)
        t_ahead_local[kept, 1] = swap_slices(imag)
        real, imag = both_spins(dagger_apply(links, 0, project(0, 1, psi)))
        t_plus[j] = to_bf16(last_slice(real, imag))
        copies[1].start()
        t_behind_local[kept, 0] = swap_slices(real)
        t_behind_local[kept, 1] = swap_slices(imag)

    def send_corners(j):
        copies = corner_copies(j)
        for i, sent in enumerate((x_minus, x_plus)):
            value = to_f32(sent[j])
            corner[j, i] = to_bf16(first_slice(value[:6], value[6:]))
            copies[i].start()
            corner[j, 2 + i] = to_bf16(last_slice(value[:6], value[6:]))
            copies[2 + i].start()

    def read_total(ref):
        return [[ref[part, s] for s in range(4)] for part in range(2)]

    def write_total(ref, result):
        for part in range(2):
            for s in range(4):
                ref[part, s] = result[part][s]

    def local_hops(kept):
        result = read_total(source)
        for direction in (2, 3):
            half = both_spins(project(direction, -1, psi))
            half = two_spins(*[ahead_of(direction, part) for part in half])
            result = add_expanded(result, direction, -1, link_apply(links, direction, half))
            half = both_spins(dagger_apply(links, direction, project(direction, 1, psi)))
            half = two_spins(*[behind_of(direction, part) for part in half])
            result = add_expanded(result, direction, 1, half)
        top = row_of((6, ROWS, LANES)) < SLICE
        half = two_spins(*[masked(top, t_ahead_local[kept, part]) for part in range(2)])
        result = add_expanded(result, 0, -1, link_apply(links, 0, half))
        half = two_spins(*[masked(~top, t_behind_local[kept, part]) for part in range(2)])
        write_total(total, add_expanded(result, 0, 1, half))

    def send_rest(k):
        copies = rest_copies(k)
        real, imag = [jnp.concatenate(part, axis=0) for part in read_total(total)]
        rest[k, 0] = to_bf16(first_slice(real, imag))
        copies[0].start()
        rest[k, 1] = to_bf16(last_slice(real, imag))
        copies[1].start()

    def receive_bulk():
        for copy in bulk_copies():
            copy.wait_recv()
        for chiral in range(2):
            real, imag = spread(to_f32(bulk_clover_in[0, chiral]), to_f32(bulk_clover_in[1, chiral]))
            clover_rim[chiral, 0] = real.reshape(6, 6, ROWS, LANES)
            clover_rim[chiral, 1] = imag.reshape(6, 6, ROWS, LANES)
        real, imag = spread(to_f32(bulk_links_in[0]), to_f32(bulk_links_in[1]))
        for direction in range(2):
            links_rim[direction, 0] = real[9 * direction : 9 * direction + 9].reshape(3, 3, ROWS, LANES)
            links_rim[direction, 1] = imag[9 * direction : 9 * direction + 9].reshape(3, 3, ROWS, LANES)

    def receive_t(j):
        copies = t_copies(j)
        top = row_of((6, ROWS, LANES)) < SLICE
        copies[0].wait_recv()
        rim = to_f32(t_ahead[j])
        halo[0, 0] = masked(~top, swap_slices(rim))
        halo[0, 1] = masked(~top, rim)
        copies[1].wait_recv()
        rim = to_f32(t_behind[j])
        halo[1, 0] = masked(top, rim)
        halo[1, 1] = masked(top, swap_slices(rim))

    def iterate_rim(k):
        kept = lax.rem(k - 1, 2)
        top = row_of((6, ROWS, LANES)) < SLICE
        zero = jnp.zeros((3, ROWS, LANES), jnp.float32)
        result = [[zero] * 4, [zero] * 4]
        half = two_spins(*[masked(top, t_behind_local[kept, part]) for part in range(2)])
        result = add_expanded(result, 0, 1, half)
        half = two_spins(*[masked(~top, t_ahead_local[kept, part]) for part in range(2)])
        result = add_expanded(result, 0, -1, link_apply(links_rim, 0, half))
        for copy in rest_copies(k):
            copy.wait_recv()
        parts = spread(to_f32(rest_in[k, 0]), to_f32(rest_in[k, 1]))
        result = [
            [result[part][s] + parts[part][3 * s : 3 * s + 3] for s in range(4)] for part in range(2)
        ]
        for copy in corner_copies(k - 1):
            copy.wait_recv()
        half = two_spins(*spread(to_f32(corner_in[k - 1, 0]), to_f32(corner_in[k - 1, 2])))
        result = add_expanded(result, 1, -1, link_apply(links_rim, 1, half))
        half = two_spins(*spread(to_f32(corner_in[k - 1, 1]), to_f32(corner_in[k - 1, 3])))
        clover_apply(clover_rim, add_expanded(result, 1, 1, half), psi_rim)
        for part, value in enumerate(both_spins(project(0, -1, psi_rim))):
            halo[0, part] = masked(~top, swap_slices(value))
        for part, value in enumerate(both_spins(dagger_apply(links_rim, 0, project(0, 1, psi_rim)))):
            halo[1, part] = masked(top, swap_slices(value))

    def with_halos(slot):
        copies = x_copies(slot)
        result = read_total(total)
        half = two_spins(halo[0, 0], halo[0, 1])
        result = add_expanded(result, 0, -1, link_apply(links, 0, half))
        result = add_expanded(result, 0, 1, two_spins(halo[1, 0], halo[1, 1]))
        copies[0].wait_recv()
        half = to_f32(x_ahead[slot])
        result = add_expanded(result, 1, -1, link_apply(links, 1, two_spins(half[:6], half[6:])))
        copies[1].wait_recv()
        half = to_f32(x_behind[slot])
        return add_expanded(result, 1, 1, two_spins(half[:6], half[6:]))

    def pack_bulk():
        for chiral in range(2):
            real = clover[chiral, 0].reshape(36, ROWS, LANES)
            imag = clover[chiral, 1].reshape(36, ROWS, LANES)
            bulk_clover[0, chiral] = to_bf16(first_slice(real, imag))
            bulk_clover[1, chiral] = to_bf16(last_slice(real, imag))
        real, imag = [
            jnp.concatenate([links[d, part].reshape(9, ROWS, LANES) for d in range(2)], axis=0)
            for part in range(2)
        ]
        bulk_links[0] = to_bf16(first_slice(real, imag))
        bulk_links[1] = to_bf16(last_slice(real, imag))

    def send_rims():
        copies = rim_copies()
        for i, (sign, field) in enumerate([(1, xi), (-1, eta)]):
            real, imag = both_spins(project(0, sign, field))
            rim_t[i] = first_slice(real, imag)
            real, imag = both_spins(project(1, sign, field))
            rim_x[i, 0] = real
            rim_x[i, 1] = imag
        for copy in copies:
            copy.start()

    def half_ahead(direction, sign, field, index):
        if direction == 1:
            return two_spins(rim_x_ahead[index, 0], rim_x_ahead[index, 1])
        real, imag = both_spins(project(direction, sign, field))
        if direction == 0:
            rim = rim_t_ahead[index]
            first = row_of(rim.shape) < SLICE
            real = jnp.where(first, swap_slices(real), swap_slices(rim))
            imag = jnp.where(first, swap_slices(imag), rim)
            return two_spins(real, imag)
        return two_spins(ahead_of(direction, real), ahead_of(direction, imag))

    def force(direction):
        outer_real = outer_imag = None
        for sign, field, index, other in ((-1, eta, 1, xi), (1, xi, 0, eta)):
            left_real, left_imag = half_ahead(direction, sign, field, index)
            right_real, right_imag = project(direction, sign, other)
            for s in range(2):
                lr, li = left_real[s][:, None], left_imag[s][:, None]
                rr, ri = right_real[s][None], right_imag[s][None]
                part_real = lr * rr + li * ri
                part_imag = li * rr - lr * ri
                outer_real = part_real if outer_real is None else outer_real + part_real
                outer_imag = part_imag if outer_imag is None else outer_imag + part_imag
        force_real = force_imag = None
        for c in range(3):
            mr, mi = gauge[direction, 0, :, c][:, None], gauge[direction, 1, :, c][:, None]
            orr, oi = outer_real[c][None], outer_imag[c][None]
            part_real = mr * orr - mi * oi
            part_imag = mr * oi + mi * orr
            force_real = part_real if c == 0 else force_real + part_real
            force_imag = part_imag if c == 0 else force_imag + part_imag
        half_step = 0.5 * step_size
        trace = (force_imag[0, 0] + force_imag[1, 1] + force_imag[2, 2]) * (step_size / 3.0)
        for a in range(3):
            updated[direction, 0, a, a] = momentum[direction, 0, a, a]
            updated[direction, 1, a, a] = momentum[direction, 1, a, a] - (
                step_size * force_imag[a, a] - trace
            )
            for b in range(a):
                anti = half_step * (force_real[a, b] - force_real[b, a])
                updated[direction, 0, a, b] = momentum[direction, 0, a, b] - anti
                updated[direction, 0, b, a] = momentum[direction, 0, b, a] + anti
                sym = half_step * (force_imag[a, b] + force_imag[b, a])
                updated[direction, 1, a, b] = momentum[direction, 1, a, b] - sym
                updated[direction, 1, b, a] = momentum[direction, 1, b, a] - sym

    loads[1].wait()
    out_row = lax.broadcasted_iota(jnp.int32, (LANES, LANES), 0)
    in_row = lax.broadcasted_iota(jnp.int32, (LANES, LANES), 1)
    place = (out_row // ROWS) * ROWS + (out_row % SLICE) * 2 + (out_row % ROWS) // SLICE
    permute = jnp.where(in_row == place, 1.0, 0.0).astype(jnp.bfloat16)
    blocks = LANES // ROWS
    for group in range(clover_low.shape[0] // LANES):
        moved = jnp.dot(
            permute, clover_low[group * LANES : (group + 1) * LANES], preferred_element_type=jnp.float32
        ).reshape(blocks, ROWS, LANES)
        for i in range(blocks):
            entry = group * blocks + i
            clover[entry // 72, entry // 36 % 2, entry // 6 % 6, entry % 6] = moved[i]
    loads[0].wait()
    clover_apply(clover, read_total(source), psi)
    loads[2].wait()
    for direction in range(4):
        for part in range(2):
            links[direction, part] = hop_scale * gauge[direction, part]
    pl.semaphore_wait(barrier, 4)
    send_t(0)
    send_x(0)
    for device in (x_next, x_last):
        pl.semaphore_signal(ready, inc=1, device_id=device, device_id_type=mesh_id)
    pack_bulk()
    for copy in bulk_copies()[:2]:
        copy.start()
    for load in loads[3:]:
        load.wait()
    pl.semaphore_wait(ready, 2)

    def iteration(k, carry):
        local_hops(lax.rem(k - 1, 2))

        @pl.when((k >= SWITCH - 1) & (k < ITERS))
        def _():
            send_rest(k)

        @pl.when(k == RIMS_AT)
        def _():
            send_rims()

        @pl.when(k == FORCE_AT)
        def _():
            for copy in rim_copies():
                copy.wait()
            for direction in range(4):
                force(direction)

        @pl.when(k < SWITCH)
        def _():
            receive_t(k - 1)

        @pl.when(k == SWITCH)
        def _():
            receive_bulk()

        @pl.when(k >= SWITCH)
        def _():
            iterate_rim(k - 1)

        clover_apply(clover, with_halos(k - 1), psi)

        @pl.when(k < SWITCH - 1)
        def _():
            send_t(k)
            send_x(k)

        @pl.when(k == 1)
        def _():
            for copy in bulk_copies()[2:]:
                copy.start()

        @pl.when((k >= SWITCH - 1) & (k < ITERS))
        def _():
            send_x(k)
            keep_t(k)

        @pl.when((k >= SWITCH - 2) & (k < ITERS - 1))
        def _():
            send_corners(k)

        return carry

    lax.fori_loop(1, ITERS + 1, iteration, 0)
    sent = bulk_copies()
    for j in range(ITERS):
        sent += x_copies(j)
        sent += t_copies(j) if j < SWITCH - 1 else []
        sent += corner_copies(j) if SWITCH - 2 <= j < ITERS - 1 else []
        sent += rest_copies(j) if j >= SWITCH - 1 else []
    for copy in sent:
        copy.wait_send()


def publish(solved, updated, solved_out, updated_out, sem):
    copies = [
        pltpu.make_async_copy(solved, solved_out, sem.at[0]),
        pltpu.make_async_copy(updated, updated_out, sem.at[1]),
    ]
    for copy in copies:
        copy.start()
    for copy in copies:
        copy.wait()


def per_device(gauge, clover_inverse, source, xi, eta, momentum):
    field = (2, 4, 3, ROWS, LANES)
    matrices = (4, 2, 3, 3, ROWS, LANES)
    half = (3, 2 * ROWS, LANES)
    full = (6, 2 * ROWS, LANES)
    chunks = LANES * SLICE // LANES
    low = clover_inverse.reshape(2, 2, 6, 6, 2, chunks, LANES)
    low = jnp.swapaxes(low, 4, 5).reshape(2 * 2 * 6 * 6 * chunks * 2, LANES)
    f32, bf16 = jnp.float32, jnp.bfloat16
    anywhere = pl.BlockSpec(memory_space=pl.ANY)
    in_hbm = pl.BlockSpec(memory_space=pltpu.HBM)
    on_chip = pl.BlockSpec(memory_space=pltpu.VMEM)
    solved, updated = pl.pallas_call(
        kernel,
        out_shape=(pltpu.VMEM(field, f32), pltpu.VMEM(matrices, f32)),
        in_specs=[anywhere] * 6,
        out_specs=(on_chip, on_chip),
        scratch_shapes=[
            pltpu.VMEM(matrices, f32),
            pltpu.VMEM(low.shape, bf16),
            pltpu.VMEM(field, f32),
            pltpu.VMEM(field, f32),
            pltpu.VMEM(field, f32),
            pltpu.VMEM(matrices, f32),
            pltpu.VMEM(matrices, f32),
            pltpu.VMEM((2, 2, 6, 6, ROWS, LANES), f32),
            pltpu.VMEM(field, f32),
            pltpu.VMEM((2, 2, 6, ROWS, LANES), f32),
            pltpu.VMEM((2, 2, 6, ROWS, LANES), f32),
            pltpu.VMEM((SWITCH - 1, *half), bf16),
            pltpu.VMEM((SWITCH - 1, *half), bf16),
            pltpu.VMEM((ITERS, *full), bf16),
            pltpu.VMEM((ITERS, *full), bf16),
            pltpu.VMEM((SWITCH - 1, *half), bf16),
            pltpu.VMEM((SWITCH - 1, *half), bf16),
            pltpu.VMEM((ITERS, *full), bf16),
            pltpu.VMEM((ITERS, *full), bf16),
            pltpu.VMEM((2, 6, ROWS, LANES), f32),
            pltpu.VMEM((2, 2, 6, ROWS, LANES), f32),
            pltpu.VMEM((2, 6, ROWS, LANES), f32),
            pltpu.VMEM((2, 2, 6, ROWS, LANES), f32),
            pltpu.VMEM((ITERS, 2, *full), bf16),
            pltpu.VMEM((ITERS, 2, *full), bf16),
            pltpu.VMEM((ITERS, 4, *half), bf16),
            pltpu.VMEM((ITERS, 4, *half), bf16),
            pltpu.VMEM((2, 2, 18, 2 * ROWS, LANES), bf16),
            pltpu.VMEM((2, 2, 18, 2 * ROWS, LANES), bf16),
            pltpu.VMEM((2, 9, 2 * ROWS, LANES), bf16),
            pltpu.VMEM((2, 9, 2 * ROWS, LANES), bf16),
            pltpu.VMEM((2, 2, 6, 6, ROWS, LANES), f32),
            pltpu.VMEM((2, 2, 3, 3, ROWS, LANES), f32),
            pltpu.VMEM(field, f32),
            pltpu.VMEM((2, 2, 6, ROWS, LANES), f32),
            pltpu.SemaphoreType.DMA((6,)),
            pltpu.SemaphoreType.DMA((10, ITERS)),
            pltpu.SemaphoreType.DMA((10, ITERS)),
            pltpu.SemaphoreType.DMA((8,)),
            pltpu.SemaphoreType.DMA((8,)),
            pltpu.SemaphoreType.REGULAR,
        ],
        compiler_params=pltpu.CompilerParams(collective_id=0, has_side_effects=True),
        name="solve",
    )(
        gauge.reshape(matrices), low, source.reshape(field), xi.reshape(field),
        eta.reshape(field), momentum.reshape(matrices),
    )
    solved, updated = pl.pallas_call(
        publish,
        out_shape=(jax.ShapeDtypeStruct(field, f32), jax.ShapeDtypeStruct(matrices, f32)),
        in_specs=[on_chip] * 2,
        out_specs=(in_hbm, in_hbm),
        scratch_shapes=[pltpu.SemaphoreType.DMA((2,))],
        compiler_params=pltpu.CompilerParams(vmem_limit_bytes=1 << 20),
        name="publish",
    )(solved, updated)
    return solved.reshape(source.shape), updated.reshape(momentum.shape)


def solution(mesh):
    spinors = P(None, None, None, "ta", "xyz", None, None)
    matrices = P(None, None, None, None, "ta", "xyz", None, None)
    return jax.shard_map(
        per_device,
        mesh=mesh,
        in_specs=(matrices, matrices, spinors, spinors, spinors, matrices),
        out_specs=(spinors, matrices),
        check_vma=False,
    )
```

```python
import functools

import jax
import jax.numpy as jnp
from jax import lax
from jax.experimental import pallas as pl
from jax.experimental.pallas import tpu as pltpu
from jax.sharding import PartitionSpec as P

NZ = 64
ITERS = 8

hop_scale = 0.18
step_size = 0.25

ROWS = 8
LANES = 128
SLICE = 4

SWITCH = 3
RIMS_AT = 4
FORCE_AT = 6


def combine(base, sign, term):
    return base + term if sign > 0 else base - term


def rotated(direction, sign, real, imag):
    if direction == 0:
        return [(sign, real[0]), (sign, real[1])], [(sign, imag[0]), (sign, imag[1])]
    if direction == 1:
        sig_real = [(1, real[1]), (1, real[0])]
        sig_imag = [(1, imag[1]), (1, imag[0])]
    elif direction == 2:
        sig_real = [(1, imag[1]), (-1, imag[0])]
        sig_imag = [(-1, real[1]), (1, real[0])]
    else:
        sig_real = [(1, real[0]), (-1, real[1])]
        sig_imag = [(1, imag[0]), (-1, imag[1])]
    return [(-sign * s, v) for s, v in sig_imag], [(sign * s, v) for s, v in sig_real]


def project(direction, sign, spinor):
    inverse_sign = sign if direction == 0 else -sign
    lower_real, lower_imag = rotated(
        direction, inverse_sign, [spinor[0, 2], spinor[0, 3]], [spinor[1, 2], spinor[1, 3]]
    )
    real = [combine(spinor[0, s], *lower_real[s]) for s in range(2)]
    imag = [combine(spinor[1, s], *lower_imag[s]) for s in range(2)]
    return real, imag


def add_expanded(total, direction, sign, half):
    real, imag = half
    lower_real, lower_imag = rotated(direction, sign, real, imag)
    new_real = [total[0][s] + real[s] for s in range(2)]
    new_real += [combine(total[0][2 + s], *lower_real[s]) for s in range(2)]
    new_imag = [total[1][s] + imag[s] for s in range(2)]
    new_imag += [combine(total[1][2 + s], *lower_imag[s]) for s in range(2)]
    return [new_real, new_imag]


def link_apply(links, direction, half):
    real, imag = half
    out_real, out_imag = [None, None], [None, None]
    for b in range(3):
        mat_real = links[direction, 0, :, b]
        mat_imag = links[direction, 1, :, b]
        for s in range(2):
            vec_real, vec_imag = real[s][b : b + 1], imag[s][b : b + 1]
            part_real = mat_real * vec_real - mat_imag * vec_imag
            part_imag = mat_real * vec_imag + mat_imag * vec_real
            out_real[s] = part_real if b == 0 else out_real[s] + part_real
            out_imag[s] = part_imag if b == 0 else out_imag[s] + part_imag
    return out_real, out_imag


def dagger_apply(links, direction, half):
    real, imag = half
    out_real, out_imag = [None, None], [None, None]
    for b in range(3):
        mat_real = links[direction, 0, b]
        mat_imag = links[direction, 1, b]
        for s in range(2):
            vec_real, vec_imag = real[s][b : b + 1], imag[s][b : b + 1]
            part_real = mat_real * vec_real + mat_imag * vec_imag
            part_imag = mat_real * vec_imag - mat_imag * vec_real
            out_real[s] = part_real if b == 0 else out_real[s] + part_real
            out_imag[s] = part_imag if b == 0 else out_imag[s] + part_imag
    return out_real, out_imag


def row_of(shape):
    return lax.broadcasted_iota(jnp.int32, shape, len(shape) - 2)


def lane_of(shape):
    return lax.broadcasted_iota(jnp.int32, shape, len(shape) - 1)


def roll(x, shift, axis):
    return pltpu.roll(x, shift, axis=x.ndim - 2 + axis)


def swap_slices(x):
    return roll(x, SLICE, 0)


def ahead_of(direction, x):
    if direction == 3:
        last = lane_of(x.shape) % NZ == NZ - 1
        return jnp.where(last, roll(x, NZ - 1, 1), roll(x, LANES - 1, 1))
    halves = roll(x, NZ, 1)
    row = row_of(x.shape) % SLICE
    next_pair = jnp.where(row == SLICE - 1, roll(halves, SLICE - 1, 0), roll(halves, ROWS - 1, 0))
    return jnp.where(lane_of(x.shape) < NZ, halves, next_pair)


def behind_of(direction, x):
    if direction == 3:
        first = lane_of(x.shape) % NZ == 0
        return jnp.where(first, roll(x, LANES - NZ + 1, 1), roll(x, 1, 1))
    halves = roll(x, NZ, 1)
    row = row_of(x.shape) % SLICE
    last_pair = jnp.where(row == 0, roll(halves, ROWS - SLICE + 1, 0), roll(halves, 1, 0))
    return jnp.where(lane_of(x.shape) < NZ, last_pair, halves)


def both_spins(half):
    return [jnp.concatenate(part, axis=0) for part in half]


def two_spins(real, imag):
    return [real[:3], real[3:]], [imag[:3], imag[3:]]


def to_bf16(x):
    return x.reshape(x.shape[0] // 2, 2 * ROWS, LANES).astype(jnp.bfloat16)


def to_f32(x):
    return x.astype(jnp.float32).reshape(2 * x.shape[0], ROWS, LANES)


def first_slice(real, imag):
    return jnp.where(row_of(real.shape) < SLICE, real, swap_slices(imag))


def last_slice(real, imag):
    return jnp.where(row_of(real.shape) < SLICE, swap_slices(real), imag)


def spread(first, last):
    top = row_of(first.shape) < SLICE
    return jnp.where(top, first, swap_slices(last)), jnp.where(top, swap_slices(first), last)


def masked(rows, part):
    return jnp.where(rows, part, 0.0)


def kernel(
    gauge_hbm, clover_hbm, source_hbm, xi_hbm, eta_hbm, momentum_hbm,
    psi, updated,
    gauge, clover_low, source, xi, eta, momentum,
    links, clover, total, t_ahead_local, t_behind_local,
    t_minus, t_plus, x_minus, x_plus,
    t_ahead, t_behind, x_ahead, x_behind,
    rim_t, rim_x, rim_t_ahead, rim_x_ahead,
    rest, rest_in, corner, corner_in, bulk_clover, bulk_clover_in, bulk_links, bulk_links_in,
    clover_rim, links_rim, psi_rim, halo,
    load_sem, send_sem, recv_sem, once_send_sem, once_recv_sem, ready,
):
    n_t, n_x = lax.axis_size("ta"), lax.axis_size("xyz")
    my_t, my_x = lax.axis_index("ta"), lax.axis_index("xyz")
    t_next, t_last = {"ta": lax.rem(my_t + 1, n_t)}, {"ta": lax.rem(my_t + n_t - 1, n_t)}
    x_next, x_last = {"xyz": lax.rem(my_x + 1, n_x)}, {"xyz": lax.rem(my_x + n_x - 1, n_x)}
    mesh_id = pl.DeviceIdType.MESH

    barrier = pltpu.get_barrier_semaphore()
    for device in (t_next, t_last, x_next, x_last):
        pl.semaphore_signal(barrier, inc=1, device_id=device, device_id_type=mesh_id)

    loads = [
        pltpu.make_async_copy(src, dst, load_sem.at[i])
        for i, (src, dst) in enumerate([
            (source_hbm, source), (clover_hbm, clover_low), (gauge_hbm, gauge),
            (xi_hbm, xi), (eta_hbm, eta), (momentum_hbm, momentum),
        ])
    ]
    for load in loads:
        load.start()

    def remote(src, dst, send, recv, device):
        return pltpu.make_async_remote_copy(
            src_ref=src, dst_ref=dst, send_sem=send, recv_sem=recv,
            device_id=device, device_id_type=mesh_id,
        )

    def slot_copy(index, slot, src, dst, device):
        return remote(src, dst, send_sem.at[index, slot], recv_sem.at[index, slot], device)

    def t_copies(slot):
        return [
            slot_copy(0, slot, t_minus.at[slot], t_ahead.at[slot], t_last),
            slot_copy(1, slot, t_plus.at[slot], t_behind.at[slot], t_next),
        ]

    def x_copies(slot):
        return [
            slot_copy(2, slot, x_minus.at[slot], x_ahead.at[slot], x_last),
            slot_copy(3, slot, x_plus.at[slot], x_behind.at[slot], x_next),
        ]

    def rest_copies(slot):
        return [
            slot_copy(4 + i, slot, rest.at[slot, i], rest_in.at[slot, i], device)
            for i, device in enumerate((t_last, t_next))
        ]

    def corner_copies(slot):
        devices = [{**t, **x} for t in (t_last, t_next) for x in (x_last, x_next)]
        return [
            slot_copy(6 + i, slot, corner.at[slot, i], corner_in.at[slot, i], device)
            for i, device in enumerate(devices)
        ]

    def once_copy(index, src, dst, device):
        return remote(src, dst, once_send_sem.at[index], once_recv_sem.at[index], device)

    def rim_copies():
        return [once_copy(0, rim_t, rim_t_ahead, t_last), once_copy(1, rim_x, rim_x_ahead, x_last)]

    def bulk_copies():
        copies = []
        for i, device in enumerate((t_last, t_next)):
            copies.append(once_copy(2 + i, bulk_clover.at[i, 0], bulk_clover_in.at[i, 0], device))
        for i, device in enumerate((t_last, t_next)):
            copies.append(once_copy(6 + i, bulk_clover.at[i, 1], bulk_clover_in.at[i, 1], device))
            copies.append(once_copy(4 + i, bulk_links.at[i], bulk_links_in.at[i], device))
        return copies

    def clover_apply(blocks, vector, out):
        for chiral in range(2):
            out_real = out_imag = None
            for j in range(6):
                spin, colour = 2 * chiral + j // 3, j % 3
                vec_real = vector[0][spin][colour : colour + 1]
                vec_imag = vector[1][spin][colour : colour + 1]
                mat_real = blocks[chiral, 0, :, j]
                mat_imag = blocks[chiral, 1, :, j]
                part_real = mat_real * vec_real - mat_imag * vec_imag
                part_imag = mat_real * vec_imag + mat_imag * vec_real
                out_real = part_real if j == 0 else out_real + part_real
                out_imag = part_imag if j == 0 else out_imag + part_imag
            for s in range(2):
                out[0, 2 * chiral + s] = out_real[3 * s : 3 * s + 3]
                out[1, 2 * chiral + s] = out_imag[3 * s : 3 * s + 3]

    def send_x(j):
        copies = x_copies(j)
        x_minus[j] = to_bf16(jnp.concatenate(both_spins(project(1, -1, psi)), axis=0))
        copies[0].start()
        x_plus[j] = to_bf16(
            jnp.concatenate(both_spins(dagger_apply(links, 1, project(1, 1, psi))), axis=0)
        )
        copies[1].start()

    def keep_t(j):
        kept = lax.rem(j, 2)
        real, imag = both_spins(project(0, -1, psi))
        t_ahead_local[kept, 0] = swap_slices(real)
        t_ahead_local[kept, 1] = swap_slices(imag)
        real, imag = both_spins(dagger_apply(links, 0, project(0, 1, psi)))
        t_behind_local[kept, 0] = swap_slices(real)
        t_behind_local[kept, 1] = swap_slices(imag)

    def send_t(j):
        kept = lax.rem(j, 2)
        copies = t_copies(j)
        real, imag = both_spins(project(0, -1, psi))
        t_minus[j] = to_bf16(first_slice(real, imag))
        copies[0].start()
        t_ahead_local[kept, 0] = swap_slices(real)
        t_ahead_local[kept, 1] = swap_slices(imag)
        real, imag = both_spins(dagger_apply(links, 0, project(0, 1, psi)))
        t_plus[j] = to_bf16(last_slice(real, imag))
        copies[1].start()
        t_behind_local[kept, 0] = swap_slices(real)
        t_behind_local[kept, 1] = swap_slices(imag)

    def pack_x(j):
        x_minus[j] = to_bf16(jnp.concatenate(both_spins(project(1, -1, psi)), axis=0))
        x_plus[j] = to_bf16(
            jnp.concatenate(both_spins(dagger_apply(links, 1, project(1, 1, psi))), axis=0)
        )

    def pack_t(j):
        kept = lax.rem(j, 2)
        real, imag = both_spins(project(0, -1, psi))
        t_minus[j] = to_bf16(first_slice(real, imag))
        t_ahead_local[kept, 0] = swap_slices(real)
        t_ahead_local[kept, 1] = swap_slices(imag)
        real, imag = both_spins(dagger_apply(links, 0, project(0, 1, psi)))
        t_plus[j] = to_bf16(last_slice(real, imag))
        t_behind_local[kept, 0] = swap_slices(real)
        t_behind_local[kept, 1] = swap_slices(imag)

    def send_corners(j):
        copies = corner_copies(j)
        for i, sent in enumerate((x_minus, x_plus)):
            value = to_f32(sent[j])
            corner[j, i] = to_bf16(first_slice(value[:6], value[6:]))
            copies[i].start()
            corner[j, 2 + i] = to_bf16(last_slice(value[:6], value[6:]))
            copies[2 + i].start()

    def read_total(ref):
        return [[ref[part, s] for s in range(4)] for part in range(2)]

    def write_total(ref, result):
        for part in range(2):
            for s in range(4):
                ref[part, s] = result[part][s]

    def local_hops(kept):
        result = read_total(source)
        for direction in (2, 3):
            half = both_spins(project(direction, -1, psi))
            half = two_spins(*[ahead_of(direction, part) for part in half])
            result = add_expanded(result, direction, -1, link_apply(links, direction, half))
            half = both_spins(dagger_apply(links, direction, project(direction, 1, psi)))
            half = two_spins(*[behind_of(direction, part) for part in half])
            result = add_expanded(result, direction, 1, half)
        top = row_of((6, ROWS, LANES)) < SLICE
        half = two_spins(*[masked(top, t_ahead_local[kept, part]) for part in range(2)])
        result = add_expanded(result, 0, -1, link_apply(links, 0, half))
        half = two_spins(*[masked(~top, t_behind_local[kept, part]) for part in range(2)])
        write_total(total, add_expanded(result, 0, 1, half))

    def send_rest(k):
        copies = rest_copies(k)
        real, imag = [jnp.concatenate(part, axis=0) for part in read_total(total)]
        rest[k, 0] = to_bf16(first_slice(real, imag))
        copies[0].start()
        rest[k, 1] = to_bf16(last_slice(real, imag))
        copies[1].start()

    def receive_bulk():
        for copy in bulk_copies():
            copy.wait_recv()
        for chiral in range(2):
            real, imag = spread(to_f32(bulk_clover_in[0, chiral]), to_f32(bulk_clover_in[1, chiral]))
            clover_rim[chiral, 0] = real.reshape(6, 6, ROWS, LANES)
            clover_rim[chiral, 1] = imag.reshape(6, 6, ROWS, LANES)
        real, imag = spread(to_f32(bulk_links_in[0]), to_f32(bulk_links_in[1]))
        for direction in range(2):
            links_rim[direction, 0] = real[9 * direction : 9 * direction + 9].reshape(3, 3, ROWS, LANES)
            links_rim[direction, 1] = imag[9 * direction : 9 * direction + 9].reshape(3, 3, ROWS, LANES)

    def receive_t(j):
        copies = t_copies(j)
        top = row_of((6, ROWS, LANES)) < SLICE
        copies[0].wait_recv()
        rim = to_f32(t_ahead[j])
        halo[0, 0] = masked(~top, swap_slices(rim))
        halo[0, 1] = masked(~top, rim)
        copies[1].wait_recv()
        rim = to_f32(t_behind[j])
        halo[1, 0] = masked(top, rim)
        halo[1, 1] = masked(top, swap_slices(rim))

    def iterate_rim(k):
        kept = lax.rem(k - 1, 2)
        top = row_of((6, ROWS, LANES)) < SLICE
        zero = jnp.zeros((3, ROWS, LANES), jnp.float32)
        result = [[zero] * 4, [zero] * 4]
        half = two_spins(*[masked(top, t_behind_local[kept, part]) for part in range(2)])
        result = add_expanded(result, 0, 1, half)
        half = two_spins(*[masked(~top, t_ahead_local[kept, part]) for part in range(2)])
        result = add_expanded(result, 0, -1, link_apply(links_rim, 0, half))
        for copy in rest_copies(k):
            copy.wait_recv()
        parts = spread(to_f32(rest_in[k, 0]), to_f32(rest_in[k, 1]))
        result = [
            [result[part][s] + parts[part][3 * s : 3 * s + 3] for s in range(4)] for part in range(2)
        ]
        for copy in corner_copies(k - 1):
            copy.wait_recv()
        half = two_spins(*spread(to_f32(corner_in[k - 1, 0]), to_f32(corner_in[k - 1, 2])))
        result = add_expanded(result, 1, -1, link_apply(links_rim, 1, half))
        half = two_spins(*spread(to_f32(corner_in[k - 1, 1]), to_f32(corner_in[k - 1, 3])))
        clover_apply(clover_rim, add_expanded(result, 1, 1, half), psi_rim)
        for part, value in enumerate(both_spins(project(0, -1, psi_rim))):
            halo[0, part] = masked(~top, swap_slices(value))
        for part, value in enumerate(both_spins(dagger_apply(links_rim, 0, project(0, 1, psi_rim)))):
            halo[1, part] = masked(top, swap_slices(value))

    def with_t(result):
        result = add_expanded(result, 0, -1, link_apply(links, 0, two_spins(halo[0, 0], halo[0, 1])))
        return add_expanded(result, 0, 1, two_spins(halo[1, 0], halo[1, 1]))

    def with_x(result, slot):
        copies = x_copies(slot)
        copies[0].wait_recv()
        half = to_f32(x_ahead[slot])
        result = add_expanded(result, 1, -1, link_apply(links, 1, two_spins(half[:6], half[6:])))
        copies[1].wait_recv()
        half = to_f32(x_behind[slot])
        return add_expanded(result, 1, 1, two_spins(half[:6], half[6:]))

    def pack_bulk():
        for chiral in range(2):
            real = clover[chiral, 0].reshape(36, ROWS, LANES)
            imag = clover[chiral, 1].reshape(36, ROWS, LANES)
            bulk_clover[0, chiral] = to_bf16(first_slice(real, imag))
            bulk_clover[1, chiral] = to_bf16(last_slice(real, imag))
        real, imag = [
            jnp.concatenate([links[d, part].reshape(9, ROWS, LANES) for d in range(2)], axis=0)
            for part in range(2)
        ]
        bulk_links[0] = to_bf16(first_slice(real, imag))
        bulk_links[1] = to_bf16(last_slice(real, imag))

    def send_rims():
        copies = rim_copies()
        for i, (sign, field) in enumerate([(1, xi), (-1, eta)]):
            real, imag = both_spins(project(0, sign, field))
            rim_t[i] = first_slice(real, imag)
            real, imag = both_spins(project(1, sign, field))
            rim_x[i, 0] = real
            rim_x[i, 1] = imag
        for copy in copies:
            copy.start()

    def half_ahead(direction, sign, field, index):
        if direction == 1:
            return two_spins(rim_x_ahead[index, 0], rim_x_ahead[index, 1])
        real, imag = both_spins(project(direction, sign, field))
        if direction == 0:
            rim = rim_t_ahead[index]
            first = row_of(rim.shape) < SLICE
            real = jnp.where(first, swap_slices(real), swap_slices(rim))
            imag = jnp.where(first, swap_slices(imag), rim)
            return two_spins(real, imag)
        return two_spins(ahead_of(direction, real), ahead_of(direction, imag))

    def force(direction):
        outer_real = outer_imag = None
        for sign, field, index, other in ((-1, eta, 1, xi), (1, xi, 0, eta)):
            left_real, left_imag = half_ahead(direction, sign, field, index)
            right_real, right_imag = project(direction, sign, other)
            for s in range(2):
                lr, li = left_real[s][:, None], left_imag[s][:, None]
                rr, ri = right_real[s][None], right_imag[s][None]
                part_real = lr * rr + li * ri
                part_imag = li * rr - lr * ri
                outer_real = part_real if outer_real is None else outer_real + part_real
                outer_imag = part_imag if outer_imag is None else outer_imag + part_imag
        force_real = force_imag = None
        for c in range(3):
            mr, mi = gauge[direction, 0, :, c][:, None], gauge[direction, 1, :, c][:, None]
            orr, oi = outer_real[c][None], outer_imag[c][None]
            part_real = mr * orr - mi * oi
            part_imag = mr * oi + mi * orr
            force_real = part_real if c == 0 else force_real + part_real
            force_imag = part_imag if c == 0 else force_imag + part_imag
        half_step = 0.5 * step_size
        trace = (force_imag[0, 0] + force_imag[1, 1] + force_imag[2, 2]) * (step_size / 3.0)
        for a in range(3):
            updated[direction, 0, a, a] = momentum[direction, 0, a, a]
            updated[direction, 1, a, a] = momentum[direction, 1, a, a] - (
                step_size * force_imag[a, a] - trace
            )
            for b in range(a):
                anti = half_step * (force_real[a, b] - force_real[b, a])
                updated[direction, 0, a, b] = momentum[direction, 0, a, b] - anti
                updated[direction, 0, b, a] = momentum[direction, 0, b, a] + anti
                sym = half_step * (force_imag[a, b] + force_imag[b, a])
                updated[direction, 1, a, b] = momentum[direction, 1, a, b] - sym
                updated[direction, 1, b, a] = momentum[direction, 1, b, a] - sym

    loads[1].wait()
    out_row = lax.broadcasted_iota(jnp.int32, (LANES, LANES), 0)
    in_row = lax.broadcasted_iota(jnp.int32, (LANES, LANES), 1)
    place = (out_row // ROWS) * ROWS + (out_row % SLICE) * 2 + (out_row % ROWS) // SLICE
    permute = jnp.where(in_row == place, 1.0, 0.0).astype(jnp.bfloat16)
    blocks = LANES // ROWS
    for group in range(clover_low.shape[0] // LANES):
        moved = jnp.dot(
            permute, clover_low[group * LANES : (group + 1) * LANES], preferred_element_type=jnp.float32
        ).reshape(blocks, ROWS, LANES)
        for i in range(blocks):
            entry = group * blocks + i
            clover[entry // 72, entry // 36 % 2, entry // 6 % 6, entry % 6] = moved[i]
    loads[0].wait()
    clover_apply(clover, read_total(source), psi)
    loads[2].wait()
    for direction in range(4):
        for part in range(2):
            links[direction, part] = hop_scale * gauge[direction, part]
    pack_t(0)
    pack_x(0)
    pl.semaphore_wait(barrier, 4)
    for copy in t_copies(0) + x_copies(0):
        copy.start()
    for device in (x_next, x_last):
        pl.semaphore_signal(ready, inc=1, device_id=device, device_id_type=mesh_id)
    pack_bulk()
    for copy in bulk_copies()[:2]:
        copy.start()
    for load in loads[3:]:
        load.wait()
    pl.semaphore_wait(ready, 2)

    def near_iteration(k):
        local_hops((k - 1) % 2)
        if k >= SWITCH - 1:
            send_rest(k)
        write_total(total, with_x(read_total(total), k - 1))
        receive_t(k - 1)
        clover_apply(clover, with_t(read_total(total)), psi)
        if k < SWITCH - 1:
            send_t(k)
            send_x(k)
        else:
            send_x(k)
            keep_t(k)
        if k == 1:
            for copy in bulk_copies()[2:]:
                copy.start()
        if k >= SWITCH - 2:
            send_corners(k)

    def far_iteration(k, last=False):
        local_hops(lax.rem(k - 1, 2))
        if not last:
            send_rest(k)

            @pl.when(k == RIMS_AT)
            def _():
                send_rims()

            @pl.when(k == FORCE_AT)
            def _():
                for copy in rim_copies():
                    copy.wait()
                for direction in range(4):
                    force(direction)

            @pl.when(k == SWITCH)
            def _():
                receive_bulk()

        iterate_rim(k - 1)
        clover_apply(clover, with_x(with_t(read_total(total)), k - 1), psi)
        if not last:
            send_x(k)
            keep_t(k)

            @pl.when(k < ITERS - 1)
            def _():
                send_corners(k)

    def looped(k, carry):
        far_iteration(k)
        return carry

    for k in range(1, SWITCH):
        near_iteration(k)
    lax.fori_loop(SWITCH, ITERS, looped, 0)
    far_iteration(ITERS, last=True)
    sent = bulk_copies()
    for j in range(ITERS):
        sent += x_copies(j)
        sent += t_copies(j) if j < SWITCH - 1 else []
        sent += corner_copies(j) if SWITCH - 2 <= j < ITERS - 1 else []
        sent += rest_copies(j) if j >= SWITCH - 1 else []
    for copy in sent:
        copy.wait_send()


def publish(solved, updated, solved_out, updated_out, sem):
    copies = [
        pltpu.make_async_copy(solved, solved_out, sem.at[0]),
        pltpu.make_async_copy(updated, updated_out, sem.at[1]),
    ]
    for copy in copies:
        copy.start()
    for copy in copies:
        copy.wait()


def per_device(gauge, clover_inverse, source, xi, eta, momentum):
    field = (2, 4, 3, ROWS, LANES)
    matrices = (4, 2, 3, 3, ROWS, LANES)
    half = (3, 2 * ROWS, LANES)
    full = (6, 2 * ROWS, LANES)
    chunks = LANES * SLICE // LANES
    low = clover_inverse.reshape(2, 2, 6, 6, 2, chunks, LANES)
    low = jnp.swapaxes(low, 4, 5).reshape(2 * 2 * 6 * 6 * chunks * 2, LANES)
    f32, bf16 = jnp.float32, jnp.bfloat16
    anywhere = pl.BlockSpec(memory_space=pl.ANY)
    in_hbm = pl.BlockSpec(memory_space=pltpu.HBM)
    on_chip = pl.BlockSpec(memory_space=pltpu.VMEM)
    solved, updated = pl.pallas_call(
        kernel,
        out_shape=(pltpu.VMEM(field, f32), pltpu.VMEM(matrices, f32)),
        in_specs=[anywhere] * 6,
        out_specs=(on_chip, on_chip),
        scratch_shapes=[
            pltpu.VMEM(matrices, f32),
            pltpu.VMEM(low.shape, bf16),
            pltpu.VMEM(field, f32),
            pltpu.VMEM(field, f32),
            pltpu.VMEM(field, f32),
            pltpu.VMEM(matrices, f32),
            pltpu.VMEM(matrices, f32),
            pltpu.VMEM((2, 2, 6, 6, ROWS, LANES), f32),
            pltpu.VMEM(field, f32),
            pltpu.VMEM((2, 2, 6, ROWS, LANES), f32),
            pltpu.VMEM((2, 2, 6, ROWS, LANES), f32),
            pltpu.VMEM((SWITCH - 1, *half), bf16),
            pltpu.VMEM((SWITCH - 1, *half), bf16),
            pltpu.VMEM((ITERS, *full), bf16),
            pltpu.VMEM((ITERS, *full), bf16),
            pltpu.VMEM((SWITCH - 1, *half), bf16),
            pltpu.VMEM((SWITCH - 1, *half), bf16),
            pltpu.VMEM((ITERS, *full), bf16),
            pltpu.VMEM((ITERS, *full), bf16),
            pltpu.VMEM((2, 6, ROWS, LANES), f32),
            pltpu.VMEM((2, 2, 6, ROWS, LANES), f32),
            pltpu.VMEM((2, 6, ROWS, LANES), f32),
            pltpu.VMEM((2, 2, 6, ROWS, LANES), f32),
            pltpu.VMEM((ITERS, 2, *full), bf16),
            pltpu.VMEM((ITERS, 2, *full), bf16),
            pltpu.VMEM((ITERS, 4, *half), bf16),
            pltpu.VMEM((ITERS, 4, *half), bf16),
            pltpu.VMEM((2, 2, 18, 2 * ROWS, LANES), bf16),
            pltpu.VMEM((2, 2, 18, 2 * ROWS, LANES), bf16),
            pltpu.VMEM((2, 9, 2 * ROWS, LANES), bf16),
            pltpu.VMEM((2, 9, 2 * ROWS, LANES), bf16),
            pltpu.VMEM((2, 2, 6, 6, ROWS, LANES), f32),
            pltpu.VMEM((2, 2, 3, 3, ROWS, LANES), f32),
            pltpu.VMEM(field, f32),
            pltpu.VMEM((2, 2, 6, ROWS, LANES), f32),
            pltpu.SemaphoreType.DMA((6,)),
            pltpu.SemaphoreType.DMA((10, ITERS)),
            pltpu.SemaphoreType.DMA((10, ITERS)),
            pltpu.SemaphoreType.DMA((8,)),
            pltpu.SemaphoreType.DMA((8,)),
            pltpu.SemaphoreType.REGULAR,
        ],
        compiler_params=pltpu.CompilerParams(collective_id=0, has_side_effects=True),
        name="solve",
    )(
        gauge.reshape(matrices), low, source.reshape(field), xi.reshape(field),
        eta.reshape(field), momentum.reshape(matrices),
    )
    solved, updated = pl.pallas_call(
        publish,
        out_shape=(jax.ShapeDtypeStruct(field, f32), jax.ShapeDtypeStruct(matrices, f32)),
        in_specs=[on_chip] * 2,
        out_specs=(in_hbm, in_hbm),
        scratch_shapes=[pltpu.SemaphoreType.DMA((2,))],
        compiler_params=pltpu.CompilerParams(vmem_limit_bytes=1 << 20),
        name="publish",
    )(solved, updated)
    return solved.reshape(source.shape), updated.reshape(momentum.shape)


def solution(mesh):
    spinors = P(None, None, None, "ta", "xyz", None, None)
    matrices = P(None, None, None, None, "ta", "xyz", None, None)
    return jax.shard_map(
        per_device,
        mesh=mesh,
        in_specs=(matrices, matrices, spinors, spinors, spinors, matrices),
        out_specs=(spinors, matrices),
        check_vma=False,
    )
```

```python
import functools

import jax
import jax.numpy as jnp
from jax import lax
from jax.experimental import pallas as pl
from jax.experimental.pallas import tpu as pltpu
from jax.sharding import PartitionSpec as P

NZ = 64
ITERS = 8

hop_scale = 0.18
step_size = 0.25

ROWS = 8
LANES = 128
SLICE = 4

SWITCH = 3
RIMS_AT = 4
FORCE_AT = 6


def combine(base, sign, term):
    return base + term if sign > 0 else base - term


def rotated(direction, sign, real, imag):
    if direction == 0:
        return [(sign, real[0]), (sign, real[1])], [(sign, imag[0]), (sign, imag[1])]
    if direction == 1:
        sig_real = [(1, real[1]), (1, real[0])]
        sig_imag = [(1, imag[1]), (1, imag[0])]
    elif direction == 2:
        sig_real = [(1, imag[1]), (-1, imag[0])]
        sig_imag = [(-1, real[1]), (1, real[0])]
    else:
        sig_real = [(1, real[0]), (-1, real[1])]
        sig_imag = [(1, imag[0]), (-1, imag[1])]
    return [(-sign * s, v) for s, v in sig_imag], [(sign * s, v) for s, v in sig_real]


def project(direction, sign, spinor):
    inverse_sign = sign if direction == 0 else -sign
    lower_real, lower_imag = rotated(
        direction, inverse_sign, [spinor[0, 2], spinor[0, 3]], [spinor[1, 2], spinor[1, 3]]
    )
    real = [combine(spinor[0, s], *lower_real[s]) for s in range(2)]
    imag = [combine(spinor[1, s], *lower_imag[s]) for s in range(2)]
    return real, imag


def add_expanded(total, direction, sign, half):
    real, imag = half
    lower_real, lower_imag = rotated(direction, sign, real, imag)
    new_real = [total[0][s] + real[s] for s in range(2)]
    new_real += [combine(total[0][2 + s], *lower_real[s]) for s in range(2)]
    new_imag = [total[1][s] + imag[s] for s in range(2)]
    new_imag += [combine(total[1][2 + s], *lower_imag[s]) for s in range(2)]
    return [new_real, new_imag]


def link_apply(links, direction, half):
    real, imag = half
    out_real, out_imag = [None, None], [None, None]
    for b in range(3):
        mat_real = links[direction, 0, :, b]
        mat_imag = links[direction, 1, :, b]
        for s in range(2):
            vec_real, vec_imag = real[s][b : b + 1], imag[s][b : b + 1]
            part_real = mat_real * vec_real - mat_imag * vec_imag
            part_imag = mat_real * vec_imag + mat_imag * vec_real
            out_real[s] = part_real if b == 0 else out_real[s] + part_real
            out_imag[s] = part_imag if b == 0 else out_imag[s] + part_imag
    return out_real, out_imag


def dagger_apply(links, direction, half):
    real, imag = half
    out_real, out_imag = [None, None], [None, None]
    for b in range(3):
        mat_real = links[direction, 0, b]
        mat_imag = links[direction, 1, b]
        for s in range(2):
            vec_real, vec_imag = real[s][b : b + 1], imag[s][b : b + 1]
            part_real = mat_real * vec_real + mat_imag * vec_imag
            part_imag = mat_real * vec_imag - mat_imag * vec_real
            out_real[s] = part_real if b == 0 else out_real[s] + part_real
            out_imag[s] = part_imag if b == 0 else out_imag[s] + part_imag
    return out_real, out_imag


def row_of(shape):
    return lax.broadcasted_iota(jnp.int32, shape, len(shape) - 2)


def lane_of(shape):
    return lax.broadcasted_iota(jnp.int32, shape, len(shape) - 1)


def roll(x, shift, axis):
    return pltpu.roll(x, shift, axis=x.ndim - 2 + axis)


def swap_slices(x):
    return roll(x, SLICE, 0)


def ahead_of(direction, x):
    if direction == 3:
        last = lane_of(x.shape) % NZ == NZ - 1
        return jnp.where(last, roll(x, NZ - 1, 1), roll(x, LANES - 1, 1))
    halves = roll(x, NZ, 1)
    row = row_of(x.shape) % SLICE
    next_pair = jnp.where(row == SLICE - 1, roll(halves, SLICE - 1, 0), roll(halves, ROWS - 1, 0))
    return jnp.where(lane_of(x.shape) < NZ, halves, next_pair)


def behind_of(direction, x):
    if direction == 3:
        first = lane_of(x.shape) % NZ == 0
        return jnp.where(first, roll(x, LANES - NZ + 1, 1), roll(x, 1, 1))
    halves = roll(x, NZ, 1)
    row = row_of(x.shape) % SLICE
    last_pair = jnp.where(row == 0, roll(halves, ROWS - SLICE + 1, 0), roll(halves, 1, 0))
    return jnp.where(lane_of(x.shape) < NZ, last_pair, halves)


def both_spins(half):
    return [jnp.concatenate(part, axis=0) for part in half]


def two_spins(real, imag):
    return [real[:3], real[3:]], [imag[:3], imag[3:]]


def to_bf16(x):
    return x.reshape(x.shape[0] // 2, 2 * ROWS, LANES).astype(jnp.bfloat16)


def to_f32(x):
    return x.astype(jnp.float32).reshape(2 * x.shape[0], ROWS, LANES)


def first_slice(real, imag):
    return jnp.where(row_of(real.shape) < SLICE, real, swap_slices(imag))


def last_slice(real, imag):
    return jnp.where(row_of(real.shape) < SLICE, swap_slices(real), imag)


def spread(first, last):
    top = row_of(first.shape) < SLICE
    return jnp.where(top, first, swap_slices(last)), jnp.where(top, swap_slices(first), last)


def masked(rows, part):
    return jnp.where(rows, part, 0.0)


def kernel(
    gauge_hbm, clover_hbm, source_hbm, xi_hbm, eta_hbm, momentum_hbm,
    psi, updated,
    gauge, clover_low, source, xi, eta, momentum,
    links, clover, total, t_ahead_local, t_behind_local,
    t_minus, t_plus, x_minus, x_plus,
    t_ahead, t_behind, x_ahead, x_behind,
    rim_t, rim_x, rim_t_ahead, rim_x_ahead,
    rest, rest_in, corner, corner_in, bulk_clover, bulk_clover_in, bulk_links, bulk_links_in,
    clover_rim, links_rim, psi_rim, halo,
    load_sem, send_sem, recv_sem, once_send_sem, once_recv_sem, ready,
):
    n_t, n_x = lax.axis_size("ta"), lax.axis_size("xyz")
    my_t, my_x = lax.axis_index("ta"), lax.axis_index("xyz")
    t_next, t_last = {"ta": lax.rem(my_t + 1, n_t)}, {"ta": lax.rem(my_t + n_t - 1, n_t)}
    x_next, x_last = {"xyz": lax.rem(my_x + 1, n_x)}, {"xyz": lax.rem(my_x + n_x - 1, n_x)}
    mesh_id = pl.DeviceIdType.MESH

    barrier = pltpu.get_barrier_semaphore()
    for device in (t_next, t_last, x_next, x_last):
        pl.semaphore_signal(barrier, inc=1, device_id=device, device_id_type=mesh_id)

    loads = [
        pltpu.make_async_copy(src, dst, load_sem.at[i])
        for i, (src, dst) in enumerate([
            (source_hbm, source), (clover_hbm, clover_low), (gauge_hbm, gauge),
            (xi_hbm, xi), (eta_hbm, eta), (momentum_hbm, momentum),
        ])
    ]
    for load in loads:
        load.start()

    def remote(src, dst, send, recv, device):
        return pltpu.make_async_remote_copy(
            src_ref=src, dst_ref=dst, send_sem=send, recv_sem=recv,
            device_id=device, device_id_type=mesh_id,
        )

    def slot_copy(index, slot, src, dst, device):
        return remote(src, dst, send_sem.at[index, slot], recv_sem.at[index, slot], device)

    def t_copies(slot):
        return [
            slot_copy(0, slot, t_minus.at[slot], t_ahead.at[slot], t_last),
            slot_copy(1, slot, t_plus.at[slot], t_behind.at[slot], t_next),
        ]

    def x_copies(slot):
        return [
            slot_copy(2, slot, x_minus.at[slot], x_ahead.at[slot], x_last),
            slot_copy(3, slot, x_plus.at[slot], x_behind.at[slot], x_next),
        ]

    def rest_copies(slot):
        return [
            slot_copy(4 + i, slot, rest.at[slot, i], rest_in.at[slot, i], device)
            for i, device in enumerate((t_last, t_next))
        ]

    def corner_copies(slot):
        devices = [{**t, **x} for t in (t_last, t_next) for x in (x_last, x_next)]
        return [
            slot_copy(6 + i, slot, corner.at[slot, i], corner_in.at[slot, i], device)
            for i, device in enumerate(devices)
        ]

    def once_copy(index, src, dst, device):
        return remote(src, dst, once_send_sem.at[index], once_recv_sem.at[index], device)

    def rim_copies():
        return [once_copy(0, rim_t, rim_t_ahead, t_last), once_copy(1, rim_x, rim_x_ahead, x_last)]

    def bulk_copies():
        copies = []
        for i, device in enumerate((t_last, t_next)):
            copies.append(once_copy(2 + i, bulk_clover.at[i, 0], bulk_clover_in.at[i, 0], device))
        for i, device in enumerate((t_last, t_next)):
            copies.append(once_copy(6 + i, bulk_clover.at[i, 1], bulk_clover_in.at[i, 1], device))
            copies.append(once_copy(4 + i, bulk_links.at[i], bulk_links_in.at[i], device))
        return copies

    def clover_apply(blocks, vector, out):
        for chiral in range(2):
            out_real = out_imag = None
            for j in range(6):
                spin, colour = 2 * chiral + j // 3, j % 3
                vec_real = vector[0][spin][colour : colour + 1]
                vec_imag = vector[1][spin][colour : colour + 1]
                mat_real = blocks[chiral, 0, :, j]
                mat_imag = blocks[chiral, 1, :, j]
                part_real = mat_real * vec_real - mat_imag * vec_imag
                part_imag = mat_real * vec_imag + mat_imag * vec_real
                out_real = part_real if j == 0 else out_real + part_real
                out_imag = part_imag if j == 0 else out_imag + part_imag
            for s in range(2):
                out[0, 2 * chiral + s] = out_real[3 * s : 3 * s + 3]
                out[1, 2 * chiral + s] = out_imag[3 * s : 3 * s + 3]

    def send_x(j):
        pack_x(j)
        for copy in x_copies(j):
            copy.start()

    def keep_t(j):
        kept = lax.rem(j, 2)
        real, imag = both_spins(project(0, -1, psi))
        t_ahead_local[kept, 0] = swap_slices(real)
        t_ahead_local[kept, 1] = swap_slices(imag)
        real, imag = both_spins(dagger_apply(links, 0, project(0, 1, psi)))
        t_behind_local[kept, 0] = swap_slices(real)
        t_behind_local[kept, 1] = swap_slices(imag)

    def send_t(j):
        kept = lax.rem(j, 2)
        copies = t_copies(j)
        real, imag = both_spins(project(0, -1, psi))
        t_minus[j] = to_bf16(first_slice(real, imag))
        copies[0].start()
        t_ahead_local[kept, 0] = swap_slices(real)
        t_ahead_local[kept, 1] = swap_slices(imag)
        real, imag = both_spins(dagger_apply(links, 0, project(0, 1, psi)))
        t_plus[j] = to_bf16(last_slice(real, imag))
        copies[1].start()
        t_behind_local[kept, 0] = swap_slices(real)
        t_behind_local[kept, 1] = swap_slices(imag)

    def pack_x(j):
        x_minus[j] = to_bf16(jnp.concatenate(both_spins(project(1, -1, psi)), axis=0))
        x_plus[j] = to_bf16(
            jnp.concatenate(both_spins(dagger_apply(links, 1, project(1, 1, psi))), axis=0)
        )

    def pack_t(j):
        kept = lax.rem(j, 2)
        real, imag = both_spins(project(0, -1, psi))
        t_minus[j] = to_bf16(first_slice(real, imag))
        t_ahead_local[kept, 0] = swap_slices(real)
        t_ahead_local[kept, 1] = swap_slices(imag)
        real, imag = both_spins(dagger_apply(links, 0, project(0, 1, psi)))
        t_plus[j] = to_bf16(last_slice(real, imag))
        t_behind_local[kept, 0] = swap_slices(real)
        t_behind_local[kept, 1] = swap_slices(imag)

    def send_corners(j):
        copies = corner_copies(j)
        for i, sent in enumerate((x_minus, x_plus)):
            value = to_f32(sent[j])
            corner[j, i] = to_bf16(first_slice(value[:6], value[6:]))
            copies[i].start()
            corner[j, 2 + i] = to_bf16(last_slice(value[:6], value[6:]))
            copies[2 + i].start()

    def read_total(ref):
        return [[ref[part, s] for s in range(4)] for part in range(2)]

    def write_total(ref, result):
        for part in range(2):
            for s in range(4):
                ref[part, s] = result[part][s]

    def local_hops(kept):
        result = read_total(source)
        for direction in (2, 3):
            half = both_spins(project(direction, -1, psi))
            half = two_spins(*[ahead_of(direction, part) for part in half])
            result = add_expanded(result, direction, -1, link_apply(links, direction, half))
            half = both_spins(dagger_apply(links, direction, project(direction, 1, psi)))
            half = two_spins(*[behind_of(direction, part) for part in half])
            result = add_expanded(result, direction, 1, half)
        top = row_of((6, ROWS, LANES)) < SLICE
        half = two_spins(*[masked(top, t_ahead_local[kept, part]) for part in range(2)])
        result = add_expanded(result, 0, -1, link_apply(links, 0, half))
        half = two_spins(*[masked(~top, t_behind_local[kept, part]) for part in range(2)])
        write_total(total, add_expanded(result, 0, 1, half))

    def send_rest(k):
        copies = rest_copies(k)
        real, imag = [jnp.concatenate(part, axis=0) for part in read_total(total)]
        rest[k, 0] = to_bf16(first_slice(real, imag))
        copies[0].start()
        rest[k, 1] = to_bf16(last_slice(real, imag))
        copies[1].start()

    def receive_bulk():
        for copy in bulk_copies():
            copy.wait_recv()
        for chiral in range(2):
            real, imag = spread(to_f32(bulk_clover_in[0, chiral]), to_f32(bulk_clover_in[1, chiral]))
            clover_rim[chiral, 0] = real.reshape(6, 6, ROWS, LANES)
            clover_rim[chiral, 1] = imag.reshape(6, 6, ROWS, LANES)
        real, imag = spread(to_f32(bulk_links_in[0]), to_f32(bulk_links_in[1]))
        for direction in range(2):
            links_rim[direction, 0] = real[9 * direction : 9 * direction + 9].reshape(3, 3, ROWS, LANES)
            links_rim[direction, 1] = imag[9 * direction : 9 * direction + 9].reshape(3, 3, ROWS, LANES)

    def receive_t(j):
        copies = t_copies(j)
        top = row_of((6, ROWS, LANES)) < SLICE
        copies[0].wait_recv()
        rim = to_f32(t_ahead[j])
        halo[0, 0] = masked(~top, swap_slices(rim))
        halo[0, 1] = masked(~top, rim)
        copies[1].wait_recv()
        rim = to_f32(t_behind[j])
        halo[1, 0] = masked(top, rim)
        halo[1, 1] = masked(top, swap_slices(rim))

    def iterate_rim(k):
        kept = lax.rem(k - 1, 2)
        top = row_of((6, ROWS, LANES)) < SLICE
        zero = jnp.zeros((3, ROWS, LANES), jnp.float32)
        result = [[zero] * 4, [zero] * 4]
        half = two_spins(*[masked(top, t_behind_local[kept, part]) for part in range(2)])
        result = add_expanded(result, 0, 1, half)
        half = two_spins(*[masked(~top, t_ahead_local[kept, part]) for part in range(2)])
        result = add_expanded(result, 0, -1, link_apply(links_rim, 0, half))
        for copy in rest_copies(k):
            copy.wait_recv()
        parts = spread(to_f32(rest_in[k, 0]), to_f32(rest_in[k, 1]))
        result = [
            [result[part][s] + parts[part][3 * s : 3 * s + 3] for s in range(4)] for part in range(2)
        ]
        for copy in corner_copies(k - 1):
            copy.wait_recv()
        half = two_spins(*spread(to_f32(corner_in[k - 1, 0]), to_f32(corner_in[k - 1, 2])))
        result = add_expanded(result, 1, -1, link_apply(links_rim, 1, half))
        half = two_spins(*spread(to_f32(corner_in[k - 1, 1]), to_f32(corner_in[k - 1, 3])))
        clover_apply(clover_rim, add_expanded(result, 1, 1, half), psi_rim)
        for part, value in enumerate(both_spins(project(0, -1, psi_rim))):
            halo[0, part] = masked(~top, swap_slices(value))
        for part, value in enumerate(both_spins(dagger_apply(links_rim, 0, project(0, 1, psi_rim)))):
            halo[1, part] = masked(top, swap_slices(value))

    def with_t(result):
        result = add_expanded(result, 0, -1, link_apply(links, 0, two_spins(halo[0, 0], halo[0, 1])))
        return add_expanded(result, 0, 1, two_spins(halo[1, 0], halo[1, 1]))

    def with_x(result, slot):
        copies = x_copies(slot)
        copies[0].wait_recv()
        copies[1].wait_recv()
        half = to_f32(x_ahead[slot])
        result = add_expanded(result, 1, -1, link_apply(links, 1, two_spins(half[:6], half[6:])))
        half = to_f32(x_behind[slot])
        return add_expanded(result, 1, 1, two_spins(half[:6], half[6:]))

    def pack_bulk():
        for chiral in range(2):
            real = clover[chiral, 0].reshape(36, ROWS, LANES)
            imag = clover[chiral, 1].reshape(36, ROWS, LANES)
            bulk_clover[0, chiral] = to_bf16(first_slice(real, imag))
            bulk_clover[1, chiral] = to_bf16(last_slice(real, imag))
        real, imag = [
            jnp.concatenate([links[d, part].reshape(9, ROWS, LANES) for d in range(2)], axis=0)
            for part in range(2)
        ]
        bulk_links[0] = to_bf16(first_slice(real, imag))
        bulk_links[1] = to_bf16(last_slice(real, imag))

    def send_rims():
        copies = rim_copies()
        for i, (sign, field) in enumerate([(1, xi), (-1, eta)]):
            real, imag = both_spins(project(0, sign, field))
            rim_t[i] = first_slice(real, imag)
            real, imag = both_spins(project(1, sign, field))
            rim_x[i, 0] = real
            rim_x[i, 1] = imag
        for copy in copies:
            copy.start()

    def half_ahead(direction, sign, field, index):
        if direction == 1:
            return two_spins(rim_x_ahead[index, 0], rim_x_ahead[index, 1])
        real, imag = both_spins(project(direction, sign, field))
        if direction == 0:
            rim = rim_t_ahead[index]
            first = row_of(rim.shape) < SLICE
            real = jnp.where(first, swap_slices(real), swap_slices(rim))
            imag = jnp.where(first, swap_slices(imag), rim)
            return two_spins(real, imag)
        return two_spins(ahead_of(direction, real), ahead_of(direction, imag))

    def force(direction):
        outer_real = outer_imag = None
        for sign, field, index, other in ((-1, eta, 1, xi), (1, xi, 0, eta)):
            left_real, left_imag = half_ahead(direction, sign, field, index)
            right_real, right_imag = project(direction, sign, other)
            for s in range(2):
                lr, li = left_real[s][:, None], left_imag[s][:, None]
                rr, ri = right_real[s][None], right_imag[s][None]
                part_real = lr * rr + li * ri
                part_imag = li * rr - lr * ri
                outer_real = part_real if outer_real is None else outer_real + part_real
                outer_imag = part_imag if outer_imag is None else outer_imag + part_imag
        force_real = force_imag = None
        for c in range(3):
            mr, mi = gauge[direction, 0, :, c][:, None], gauge[direction, 1, :, c][:, None]
            orr, oi = outer_real[c][None], outer_imag[c][None]
            part_real = mr * orr - mi * oi
            part_imag = mr * oi + mi * orr
            force_real = part_real if c == 0 else force_real + part_real
            force_imag = part_imag if c == 0 else force_imag + part_imag
        half_step = 0.5 * step_size
        trace = (force_imag[0, 0] + force_imag[1, 1] + force_imag[2, 2]) * (step_size / 3.0)
        for a in range(3):
            updated[direction, 0, a, a] = momentum[direction, 0, a, a]
            updated[direction, 1, a, a] = momentum[direction, 1, a, a] - (
                step_size * force_imag[a, a] - trace
            )
            for b in range(a):
                anti = half_step * (force_real[a, b] - force_real[b, a])
                updated[direction, 0, a, b] = momentum[direction, 0, a, b] - anti
                updated[direction, 0, b, a] = momentum[direction, 0, b, a] + anti
                sym = half_step * (force_imag[a, b] + force_imag[b, a])
                updated[direction, 1, a, b] = momentum[direction, 1, a, b] - sym
                updated[direction, 1, b, a] = momentum[direction, 1, b, a] - sym

    loads[1].wait()
    out_row = lax.broadcasted_iota(jnp.int32, (LANES, LANES), 0)
    in_row = lax.broadcasted_iota(jnp.int32, (LANES, LANES), 1)
    place = (out_row // ROWS) * ROWS + (out_row % SLICE) * 2 + (out_row % ROWS) // SLICE
    permute = jnp.where(in_row == place, 1.0, 0.0).astype(jnp.bfloat16)
    blocks = LANES // ROWS
    for group in range(clover_low.shape[0] // LANES):
        moved = jnp.dot(
            permute, clover_low[group * LANES : (group + 1) * LANES], preferred_element_type=jnp.float32
        ).reshape(blocks, ROWS, LANES)
        for i in range(blocks):
            entry = group * blocks + i
            clover[entry // 72, entry // 36 % 2, entry // 6 % 6, entry % 6] = moved[i]
    loads[0].wait()
    clover_apply(clover, read_total(source), psi)
    loads[2].wait()
    for direction in range(4):
        for part in range(2):
            links[direction, part] = hop_scale * gauge[direction, part]
    pack_t(0)
    pack_x(0)
    pl.semaphore_wait(barrier, 4)
    for copy in t_copies(0) + x_copies(0):
        copy.start()
    for device in (x_next, x_last):
        pl.semaphore_signal(ready, inc=1, device_id=device, device_id_type=mesh_id)
    pack_bulk()
    for copy in bulk_copies()[:2]:
        copy.start()
    for load in loads[3:]:
        load.wait()
    pl.semaphore_wait(ready, 2)

    def near_iteration(k):
        local_hops((k - 1) % 2)
        if k >= SWITCH - 1:
            send_rest(k)
        write_total(total, with_x(read_total(total), k - 1))
        receive_t(k - 1)
        clover_apply(clover, with_t(read_total(total)), psi)
        if k < SWITCH - 1:
            send_t(k)
            send_x(k)
        else:
            send_x(k)
            keep_t(k)
        if k == 1:
            for copy in bulk_copies()[2:]:
                copy.start()
        if k >= SWITCH - 2:
            send_corners(k)

    def far_iteration(k, last=False):
        local_hops(lax.rem(k - 1, 2))
        if not last:
            send_rest(k)

            @pl.when(k == RIMS_AT)
            def _():
                send_rims()

            @pl.when(k == FORCE_AT)
            def _():
                for copy in rim_copies():
                    copy.wait()
                for direction in range(4):
                    force(direction)

            @pl.when(k == SWITCH)
            def _():
                receive_bulk()

        iterate_rim(k - 1)
        clover_apply(clover, with_x(with_t(read_total(total)), k - 1), psi)
        if not last:
            send_x(k)
            keep_t(k)

            @pl.when(k < ITERS - 1)
            def _():
                send_corners(k)

    def looped(k, carry):
        far_iteration(k)
        return carry

    for k in range(1, SWITCH):
        near_iteration(k)
    lax.fori_loop(SWITCH, ITERS, looped, 0)
    far_iteration(ITERS, last=True)
    sent = bulk_copies()
    for j in range(ITERS):
        sent += x_copies(j)
        sent += t_copies(j) if j < SWITCH - 1 else []
        sent += corner_copies(j) if SWITCH - 2 <= j < ITERS - 1 else []
        sent += rest_copies(j) if j >= SWITCH - 1 else []
    for copy in sent:
        copy.wait_send()


def publish(solved, updated, solved_out, updated_out, sem):
    copies = [
        pltpu.make_async_copy(solved, solved_out, sem.at[0]),
        pltpu.make_async_copy(updated, updated_out, sem.at[1]),
    ]
    for copy in copies:
        copy.start()
    for copy in copies:
        copy.wait()


def per_device(gauge, clover_inverse, source, xi, eta, momentum):
    field = (2, 4, 3, ROWS, LANES)
    matrices = (4, 2, 3, 3, ROWS, LANES)
    half = (3, 2 * ROWS, LANES)
    full = (6, 2 * ROWS, LANES)
    chunks = LANES * SLICE // LANES
    low = clover_inverse.reshape(2, 2, 6, 6, 2, chunks, LANES)
    low = jnp.swapaxes(low, 4, 5).reshape(2 * 2 * 6 * 6 * chunks * 2, LANES)
    f32, bf16 = jnp.float32, jnp.bfloat16
    anywhere = pl.BlockSpec(memory_space=pl.ANY)
    in_hbm = pl.BlockSpec(memory_space=pltpu.HBM)
    on_chip = pl.BlockSpec(memory_space=pltpu.VMEM)
    solved, updated = pl.pallas_call(
        kernel,
        out_shape=(pltpu.VMEM(field, f32), pltpu.VMEM(matrices, f32)),
        in_specs=[anywhere] * 6,
        out_specs=(on_chip, on_chip),
        scratch_shapes=[
            pltpu.VMEM(matrices, f32),
            pltpu.VMEM(low.shape, bf16),
            pltpu.VMEM(field, f32),
            pltpu.VMEM(field, f32),
            pltpu.VMEM(field, f32),
            pltpu.VMEM(matrices, f32),
            pltpu.VMEM(matrices, f32),
            pltpu.VMEM((2, 2, 6, 6, ROWS, LANES), f32),
            pltpu.VMEM(field, f32),
            pltpu.VMEM((2, 2, 6, ROWS, LANES), f32),
            pltpu.VMEM((2, 2, 6, ROWS, LANES), f32),
            pltpu.VMEM((SWITCH - 1, *half), bf16),
            pltpu.VMEM((SWITCH - 1, *half), bf16),
            pltpu.VMEM((ITERS, *full), bf16),
            pltpu.VMEM((ITERS, *full), bf16),
            pltpu.VMEM((SWITCH - 1, *half), bf16),
            pltpu.VMEM((SWITCH - 1, *half), bf16),
            pltpu.VMEM((ITERS, *full), bf16),
            pltpu.VMEM((ITERS, *full), bf16),
            pltpu.VMEM((2, 6, ROWS, LANES), f32),
            pltpu.VMEM((2, 2, 6, ROWS, LANES), f32),
            pltpu.VMEM((2, 6, ROWS, LANES), f32),
            pltpu.VMEM((2, 2, 6, ROWS, LANES), f32),
            pltpu.VMEM((ITERS, 2, *full), bf16),
            pltpu.VMEM((ITERS, 2, *full), bf16),
            pltpu.VMEM((ITERS, 4, *half), bf16),
            pltpu.VMEM((ITERS, 4, *half), bf16),
            pltpu.VMEM((2, 2, 18, 2 * ROWS, LANES), bf16),
            pltpu.VMEM((2, 2, 18, 2 * ROWS, LANES), bf16),
            pltpu.VMEM((2, 9, 2 * ROWS, LANES), bf16),
            pltpu.VMEM((2, 9, 2 * ROWS, LANES), bf16),
            pltpu.VMEM((2, 2, 6, 6, ROWS, LANES), f32),
            pltpu.VMEM((2, 2, 3, 3, ROWS, LANES), f32),
            pltpu.VMEM(field, f32),
            pltpu.VMEM((2, 2, 6, ROWS, LANES), f32),
            pltpu.SemaphoreType.DMA((6,)),
            pltpu.SemaphoreType.DMA((10, ITERS)),
            pltpu.SemaphoreType.DMA((10, ITERS)),
            pltpu.SemaphoreType.DMA((8,)),
            pltpu.SemaphoreType.DMA((8,)),
            pltpu.SemaphoreType.REGULAR,
        ],
        compiler_params=pltpu.CompilerParams(collective_id=0, has_side_effects=True),
        name="solve",
    )(
        gauge.reshape(matrices), low, source.reshape(field), xi.reshape(field),
        eta.reshape(field), momentum.reshape(matrices),
    )
    solved, updated = pl.pallas_call(
        publish,
        out_shape=(jax.ShapeDtypeStruct(field, f32), jax.ShapeDtypeStruct(matrices, f32)),
        in_specs=[on_chip] * 2,
        out_specs=(in_hbm, in_hbm),
        scratch_shapes=[pltpu.SemaphoreType.DMA((2,))],
        compiler_params=pltpu.CompilerParams(vmem_limit_bytes=1 << 20),
        name="publish",
    )(solved, updated)
    return solved.reshape(source.shape), updated.reshape(momentum.shape)


def solution(mesh):
    spinors = P(None, None, None, "ta", "xyz", None, None)
    matrices = P(None, None, None, None, "ta", "xyz", None, None)
    return jax.shard_map(
        per_device,
        mesh=mesh,
        in_specs=(matrices, matrices, spinors, spinors, spinors, matrices),
        out_specs=(spinors, matrices),
        check_vma=False,
    )
```
